512 devices in a mesh: pole: 16 (over x, z_lo, core), slab: 32 (over y, z_hi).
Axes of the slice: x: 4, y: 8, z: 8 (z_hi: 4, z_lo: 2; z = z_hi * 2 + z_lo), core: 2. Of those that a mesh axis runs over, the one named last changes fastest.
Arguments:
- vectors: float32 [2, 16, 128, 16, 128], P(None, None, 'slab'), may hold values from -6 to 6
- potential: float32 [128, 16, 128], P('slab'), may hold values from 0 to 2
Outputs:
- filtered: float32 [2, 16, 128, 16, 128], P(None, None, 'slab', 'pole')
- gram_correlation: float32 [2, 16, 16], replicated
- gram_energy: float32 [2, 16, 16], replicated
The draws below stay inside these ranges and needn't reach their ends.
All inputs are finite; a program needn't handle non-finite values.
Results may differ from the reference program's by a relative error of at most 0.005.
Values sent between devices are 32-bit elements; how exact they have to be, the bound alone decides.
No kernel may reach another device: no remote copies, remote signals or barrier semaphores. Data moves between devices by JAX's collectives and lax.ppermute only.
A program may use at most 64 MiB of HBM per device.

```python
import math
import jax
import jax.numpy as jnp
from jax import lax

NB = 16
NX = 16
NY = 128
ITERS = 3
POLES = 16
NZ = 128


def shard_levels(own_key, shape, pieces, low, largest):
    gain, own = 1.0, jax.random.fold_in(own_key, 6)
    for dim, blocks in pieces:
        draws = jnp.exp(jax.random.uniform(jax.random.fold_in(own, dim), (blocks,), jnp.float32, low / len(pieces), largest / len(pieces)))
        gain = gain * jnp.repeat(draws, shape[dim] // blocks).reshape([-1 if axis == dim else 1 for axis in range(len(shape))])
    return gain


def normal_values(stream_key, extent, width, reach, split=(), kind=jnp.bfloat16):
    gain = shard_levels(stream_key, extent, split, -0.22, 0.18) if split else 1.0
    array = jax.random.normal(stream_key, extent, jnp.float32) * width * gain
    return jnp.minimum(jnp.maximum(array, -reach), reach).astype(kind)


def setup_inputs(seed: int = 0) -> dict:
    splits = jax.random.split(jax.random.key(seed), 3)
    return {
        "vectors": normal_values(splits[0], (2, NB, NZ, NX, NY), 1.0, 6.0, ((2, 32),), jnp.float32),
        "potential": jnp.clip(2.0 * jax.random.uniform(splits[1], (NZ, NX, NY), jnp.float32) ** shard_levels(splits[1], (NZ, NX, NY), ((0, 32),), -0.2, 0.2), 0.0, 2.0),
    }


contour_center = 2.0
contour_radius = 1.5


def apply_shifted(block, potential, shift_re, shift_im):
    beside = jnp.roll(block, 1, 2) + jnp.roll(block, -1, 2)
    beside = beside + jnp.roll(block, 1, 3) + jnp.roll(block, -1, 3)
    beside = beside + jnp.roll(block, 1, 4) + jnp.roll(block, -1, 4)
    diagonal = shift_re - 3.0 - potential
    real_part = diagonal * block[0] - shift_im * block[1] + 0.5 * beside[0]
    imag_part = diagonal * block[1] + shift_im * block[0] + 0.5 * beside[1]
    return jnp.stack([real_part, imag_part])


def bilinear(left, right):
    real_part = jnp.sum(left[0] * right[0] - left[1] * right[1], axis=(1, 2, 3))
    imag_part = jnp.sum(left[0] * right[1] + left[1] * right[0], axis=(1, 2, 3))
    return jnp.stack([real_part, imag_part])


def complex_divide(numer, denom):
    magnitude = denom[0] * denom[0] + denom[1] * denom[1]
    return jnp.stack([(numer[0] * denom[0] + numer[1] * denom[1]) / magnitude,
                      (numer[1] * denom[0] - numer[0] * denom[1]) / magnitude])


def column_scale(coef, block):
    first = coef[0][:, None, None, None]
    second = coef[1][:, None, None, None]
    return jnp.stack([first * block[0] - second * block[1], first * block[1] + second * block[0]])


def scalar_scale(first, second, block):
    return jnp.stack([first * block[0] - second * block[1], first * block[1] + second * block[0]])


def inner(left, right):
    return lax.dot_general(left, right, (((1,), (1,)), ((), ())), precision=lax.Precision.HIGHEST,
                           preferred_element_type=jnp.float32)


def gram_pair(filtered, image, cells):
    count = filtered.shape[1]
    sre = filtered[0].reshape(count, -1)
    sim = filtered[1].reshape(count, -1)
    hre = image[0].reshape(count, -1)
    him = image[1].reshape(count, -1)
    correlation = jnp.stack([inner(sre, sre) + inner(sim, sim), inner(sre, sim) - inner(sim, sre)]) / cells
    energy = jnp.stack([inner(sre, hre) + inner(sim, him), inner(sre, him) - inner(sim, hre)]) / cells
    return correlation, energy


def reference(vectors, potential):
    angles = (2.0 * math.pi / POLES) * (jnp.arange(POLES, dtype=jnp.float32) + 0.5)
    cosines = jnp.cos(angles)
    sines = jnp.sin(angles)
    start = vectors
    filtered = jnp.zeros_like(start)
    image = jnp.zeros_like(start)
    for pole_id in range(POLES):
        shift_re = contour_center + contour_radius * cosines[pole_id]
        shift_im = contour_radius * sines[pole_id]
        weight_re = contour_radius * cosines[pole_id] / POLES
        weight_im = contour_radius * sines[pole_id] / POLES
        solution = jnp.zeros_like(start)
        residual = start
        direction = start
        rho = bilinear(residual, residual)
        for iteration in range(ITERS):
            mapped = apply_shifted(direction, potential, shift_re, shift_im)
            alpha = complex_divide(rho, bilinear(direction, mapped))
            solution = solution + column_scale(alpha, direction)
            residual = residual - column_scale(alpha, mapped)
            if iteration + 1 < ITERS:
                rho_new = bilinear(residual, residual)
                direction = residual + column_scale(complex_divide(rho_new, rho), direction)
                rho = rho_new
        filtered = filtered + scalar_scale(weight_re, weight_im, solution)
        hsol = scalar_scale(shift_re, shift_im, solution) - start + residual
        image = image + scalar_scale(weight_re, weight_im, hsol)
    correlation, energy = gram_pair(filtered, image, NZ * NX * NY)
    return filtered, correlation, energy
```

```python
import functools
import math

import jax
import jax.numpy as jnp
from jax import lax
from jax.experimental import pallas as pl
from jax.experimental.pallas import tpu as pltpu
from jax.sharding import Mesh
from jax.sharding import PartitionSpec as P

contour_center = 2.0
contour_radius = 1.5
BASE = 4.0
NB = 16
ROWS = 2 * NB
NZ = 4
NX = 16
WIDE = (-2, -1, 0, 1, 2, 3)
UPPER = [(0, k) for k in (-2, -1, 0, 1, 2)] + [(1, k) for k in (-1, 0, 1)] + [(2, 0)]
LOWER = [(3, k) for k in (-1, 0, 1, 2)] + [(2, k) for k in (0, 1)]
UPPER_POT = [(0, -1), (0, 0), (0, 1), (1, 0)]
LOWER_POT = [(3, 0), (3, 1)]
PHASES = (("core", "y"), ("x", "zlo", "zhi"))
POLE = ("x", "zlo", "core")
SLAB = ("y", "zhi")


def own_row():
    return lax.axis_index(POLE)


def gather_rows(row_ref, vectors, potential, own, up, down, sems):
    row = row_ref[0]
    copies = []
    for z in range(NZ):
        for k in WIDE:
            at = lax.rem(row + (k + NX), NX)
            slot = z * len(WIDE) + k + 2
            copy = pltpu.make_async_copy(vectors.at[:, :, z, at, :], own.at[slot], sems.at[slot])
            copy.start()
            copies.append(copy)
    for copy in copies:
        copy.wait()

    def send(out, cells, levels):
        for i, (z, k) in enumerate(cells):
            block = own[z * len(WIDE) + k + 2]
            out[pl.ds(i * ROWS, ROWS), :] = block.reshape(ROWS, 128)
        for i, (z, k) in enumerate(levels):
            at = lax.rem(row + (k + NX), NX)
            out[pl.ds(len(cells) * ROWS + i, 1), :] = potential[z, pl.ds(at, 1), :]
        rest = 8 - len(levels)
        out[pl.ds(len(cells) * ROWS + len(levels), rest), :] = jnp.zeros((rest, 128), jnp.float32)

    send(down, UPPER, UPPER_POT)
    send(up, LOWER, LOWER_POT)


def krylov_gram(row_ref, own, above, below, potential, packed, fields, stack):
    row = row_ref[0]
    v0, diag = {}, {}
    for z in range(NZ):
        for k in WIDE:
            v0[z, k] = own[z * len(WIDE) + k + 2].reshape(ROWS, 128)
        for k in (-1, 0, 1, 2):
            at = lax.rem(row + (k + NX), NX)
            diag[z, k] = potential[z, pl.ds(at, 1), :] + (3.0 - BASE)
    for i, (z, k) in enumerate(UPPER):
        v0[z + NZ, k] = above[pl.ds(i * ROWS, ROWS), :]
    for i, (z, k) in enumerate(UPPER_POT):
        diag[z + NZ, k] = above[pl.ds(len(UPPER) * ROWS + i, 1), :] + (3.0 - BASE)
    for i, (z, k) in enumerate(LOWER):
        v0[z - NZ, k] = below[pl.ds(i * ROWS, ROWS), :]
    for i, (z, k) in enumerate(LOWER_POT):
        diag[z - NZ, k] = below[pl.ds(len(LOWER) * ROWS + i, 1), :] + (3.0 - BASE)

    def apply(v, z, k):
        here = v[z, k]
        beside = v[z - 1, k] + v[z + 1, k] + (v[z, k - 1] + v[z, k + 1])
        beside = beside + (pltpu.roll(here, 1, 1) + pltpu.roll(here, 127, 1))
        return diag[z, k] * here - 0.5 * beside

    v1, v2 = {}, {}
    for z, k in (
        [(z, 0) for z in range(-1, 6)]
        + [(z, 1) for z in range(-1, 5)]
        + [(z, -1) for z in range(0, 5)]
        + [(z, 2) for z in range(0, 4)]
    ):
        v1[z, k] = apply(v0, z, k)
    for z, k in [(z, 0) for z in range(0, 5)] + [(z, 1) for z in range(0, 4)]:
        v2[z, k] = apply(v1, z, k)
    for z in range(NZ):
        here = v2[z, 0]
        ahead = v2[z + 1, 0] + v2[z, 1] + pltpu.roll(here, 127, 1)
        half = 0.5 * (diag[z, 0] * here - ahead)
        for i, block in enumerate((v0[z, 0], v1[z, 0], here)):
            fields[z, pl.ds(i * ROWS, ROWS), :] = block
            stack[pl.ds(i * ROWS, ROWS), pl.ds(z * 128, 128)] = block
        stack[pl.ds(3 * ROWS, ROWS), pl.ds(z * 128, 128)] = half
    gram = lax.dot_general(
        stack[...],
        stack[...],
        (((1,), (1,)), ((), ())),
        precision=lax.Precision.HIGHEST,
        preferred_element_type=jnp.float32,
    )
    lane = lax.broadcasted_iota(jnp.int32, (NB, 128), 1)
    sub = lax.broadcasted_iota(jnp.int32, (NB, 128), 0)
    result = jnp.zeros((NB, 128), jnp.float32)
    blocks = [[(0, 0)], [(0, 1)], [(1, 1)], [(1, 2)], [(2, 2)], [(2, 3), (3, 2)]]
    for n, parts in enumerate(blocks):
        rr = ri = ir = ii = 0.0
        for i, j in parts:
            top = gram[ROWS * i : ROWS * i + NB, :]
            low = gram[ROWS * i + NB : ROWS * i + ROWS, :]
            first = (NB * n - ROWS * j) % 128
            second = (NB * n - ROWS * j - NB) % 128
            rr = rr + (pltpu.roll(top, first, 1) if first else top)
            ri = ri + (pltpu.roll(top, second, 1) if second else top)
            ir = ir + (pltpu.roll(low, first, 1) if first else low)
            ii = ii + (pltpu.roll(low, second, 1) if second else low)
        col = lane - NB * n
        inside = (col >= 0) & (col < NB)
        result = jnp.where(inside, jnp.where(col >= sub, rr + ii, ri - ir), result)
        on = col == sub
        m_re = jnp.sum(jnp.where(on, rr - ii, 0.0), axis=1, keepdims=True)
        m_im = jnp.sum(jnp.where(on, ri + ir, 0.0), axis=1, keepdims=True)
        result = jnp.where(lane == 6 * NB + 2 * n, m_re, result)
        result = jnp.where(lane == 6 * NB + 2 * n + 1, m_im, result)
    packed[...] = result


def cmul(a, b):
    return (a[0] * b[0] - a[1] * b[1], a[0] * b[1] + a[1] * b[0])


def cadd(a, b):
    return (a[0] + b[0], a[1] + b[1])


def csub(a, b):
    return (a[0] - b[0], a[1] - b[1])


def cdiv(a, b):
    size = b[0] * b[0] + b[1] * b[1]
    return ((a[0] * b[0] + a[1] * b[1]) / size, (a[1] * b[0] - a[0] * b[1]) / size)


def combine(poles, cells, parts, total, fields, filtered, correlation, energy):
    moments = total[...]
    lane = lax.broadcasted_iota(jnp.int32, (NB, 128), 1)
    m = [
        tuple(
            jnp.broadcast_to(moments[:, 6 * NB + 2 * n + c : 6 * NB + 2 * n + c + 1], (NB, 128))
            for c in (0, 1)
        )
        for n in range(6)
    ]
    cosine = jnp.zeros((NB, 128), jnp.float32)
    sine = jnp.zeros((NB, 128), jnp.float32)
    for j in range(poles):
        angle = 2.0 * math.pi / poles * (j + 0.5)
        cosine = jnp.where(lane == j, math.cos(angle), cosine)
        sine = jnp.where(lane == j, math.sin(angle), sine)
    shift = (contour_center + contour_radius * cosine, contour_radius * sine)
    weight = (contour_radius * cosine / poles, contour_radius * sine / poles)
    zeta = (shift[0] - BASE, shift[1])

    def form(p, q):
        sums = {}
        for i, a in enumerate(p):
            for j, b in enumerate(q):
                ab = cmul(a, b)
                sums[i + j] = cadd(sums[i + j], ab) if i + j in sums else ab
        out = None
        for n, s in sums.items():
            term = cmul(s, m[n])
            out = term if out is None else cadd(out, term)
        return out

    def applied(p):
        q = [cmul(zeta, a) for a in p]
        q = [q[0]] + [csub(q[i], p[i - 1]) for i in range(1, len(p))]
        return q + [(-p[-1][0], -p[-1][1])]

    one = (jnp.ones((NB, 128), jnp.float32), jnp.zeros((NB, 128), jnp.float32))
    residual, direction, solution_ = [one], [one], []
    rho = m[0]
    for iteration in range(3):
        q = applied(direction)
        alpha = cdiv(rho, form(direction, q))
        step = [cmul(alpha, d) for d in direction]
        solution_ = [cadd(s, t) for s, t in zip(solution_, step)] + step[len(solution_) :]
        step = [cmul(alpha, d) for d in q]
        residual = [csub(r, t) for r, t in zip(residual, step)] + [
            (-t[0], -t[1]) for t in step[len(residual) :]
        ]
        if iteration < 2:
            rho_new = form(residual, residual)
            beta = cdiv(rho_new, rho)
            step = [cmul(beta, d) for d in direction]
            direction = [cadd(r, t) for r, t in zip(residual, step)] + residual[len(step) :]
            rho = rho_new
    image = []
    for k in range(4):
        term = residual[k]
        if k < 3:
            term = cadd(term, cmul(shift, solution_[k]))
        if k == 0:
            term = (term[0] - 1.0, term[1])
        image.append(term)

    def over_poles(term):
        term = cmul(weight, term)
        return tuple(
            jnp.sum(jnp.where(lane < poles, t, 0.0), axis=1, keepdims=True) for t in term
        )

    coef = [over_poles(s) for s in solution_]
    coef_image = [over_poles(s) for s in image]
    for z in range(NZ):
        re = im = 0.0
        for k in range(3):
            v_re = fields[z, pl.ds(k * ROWS, NB), :]
            v_im = fields[z, pl.ds(k * ROWS + NB, NB), :]
            re = re + (coef[k][0] * v_re - coef[k][1] * v_im)
            im = im + (coef[k][0] * v_im + coef[k][1] * v_re)
        filtered[0, :, z, :] = re
        filtered[1, :, z, :] = im

    a = lax.broadcasted_iota(jnp.int32, (NB, NB), 0)
    b = lax.broadcasted_iota(jnp.int32, (NB, NB), 1)
    flipped = lax.dot_general(
        moments,
        jnp.where(a == b, 1.0, 0.0),
        (((0,), (0,)), ((), ())),
        precision=lax.Precision.HIGHEST,
        preferred_element_type=jnp.float32,
    )
    inner = []
    for n in range(6):
        here = moments[:, NB * n : NB * n + NB]
        there = flipped[NB * n : NB * n + NB, :]
        inner.append(
            (
                jnp.where(b >= a, here, there),
                jnp.where(b < a, here, jnp.where(b > a, -there, 0.0)),
            )
        )

    def as_row(c):
        return tuple(
            jnp.sum(jnp.where(a == b, jnp.broadcast_to(t, (NB, NB)), 0.0), axis=0, keepdims=True)
            for t in c
        )

    def product(right, out):
        rows = [as_row(c) for c in right]
        result = None
        for k in range(3):
            part = None
            for l, r in enumerate(rows):
                term = cmul(r, inner[k + l])
                part = term if part is None else cadd(part, term)
            term = cmul((coef[k][0], -coef[k][1]), part)
            result = term if result is None else cadd(result, term)
        out[0] = result[0] * (1.0 / cells)
        out[1] = result[1] * (1.0 / cells)

    product(coef, correlation)
    product(coef_image, energy)


def on_device(vectors, potential):
    f32 = jnp.float32
    vmem = pl.BlockSpec(memory_space=pltpu.VMEM)
    smem = pl.BlockSpec(memory_space=pltpu.SMEM)
    row = own_row().reshape(1).astype(jnp.int32)
    slots = NZ * len(WIDE)
    own, up, down = pl.pallas_call(
        gather_rows,
        in_specs=[smem, pl.BlockSpec(memory_space=pl.ANY), vmem],
        out_specs=[vmem] * 3,
        out_shape=[
            jax.ShapeDtypeStruct((slots, 2, NB, 128), f32),
            jax.ShapeDtypeStruct((len(LOWER) * ROWS + 8, 128), f32),
            jax.ShapeDtypeStruct((len(UPPER) * ROWS + 8, 128), f32),
        ],
        scratch_shapes=[pltpu.SemaphoreType.DMA((slots,))],
        name="gather_rows",
    )(row, vectors, potential)
    slabs = lax.axis_size(SLAB)
    ahead = [(i, (i + 1) % slabs) for i in range(slabs)]
    back = [(i, (i - 1) % slabs) for i in range(slabs)]
    above = lax.ppermute(down, SLAB, back)
    below = lax.ppermute(up, SLAB, ahead)
    packed, fields = pl.pallas_call(
        krylov_gram,
        in_specs=[smem] + [vmem] * 4,
        out_specs=[vmem] * 2,
        out_shape=[
            jax.ShapeDtypeStruct((NB, 128), f32),
            jax.ShapeDtypeStruct((NZ, 3 * ROWS, 128), f32),
        ],
        scratch_shapes=[pltpu.VMEM((4 * ROWS, NZ * 128), f32)],
        name="krylov_gram",
    )(row, own, above, below, potential)
    for axes in PHASES:
        count = lax.axis_size(axes)
        shared = jnp.broadcast_to(packed[None], (count, NB, 128))
        packed = jnp.sum(lax.all_to_all(shared, axes, 0, 0), axis=0)
    cells = NZ * slabs * NX * 128
    filtered, correlation, energy = pl.pallas_call(
        functools.partial(combine, lax.axis_size(POLE), cells, None),
        in_specs=[vmem] * 2,
        out_specs=[vmem] * 3,
        out_shape=[
            jax.ShapeDtypeStruct((2, NB, NZ, 128), f32),
            jax.ShapeDtypeStruct((2, NB, NB), f32),
            jax.ShapeDtypeStruct((2, NB, NB), f32),
        ],
        name="combine",
    )(packed, fields)
    return filtered[:, :, :, None, :], correlation, energy


def solution(mesh):
    fine = Mesh(mesh.devices.reshape(4, 2, 2, 8, 4), POLE + SLAB)
    in_specs = (P(None, None, SLAB, None, None), P(SLAB, None, None))
    out_specs = (P(None, None, SLAB, POLE, None), P(), P())
    return jax.shard_map(
        on_device, mesh=fine, in_specs=in_specs, out_specs=out_specs, check_vma=False
    )
```

```python
import functools
import math

import jax
import jax.numpy as jnp
from jax import lax
from jax.experimental import pallas as pl
from jax.experimental.pallas import tpu as pltpu
from jax.sharding import Mesh
from jax.sharding import PartitionSpec as P

contour_center = 2.0
contour_radius = 1.5
BASE = 4.0
NB = 16
ROWS = 2 * NB
NZ = 4
NX = 16
WIDE = (-2, -1, 0, 1, 2, 3)
LOWER = [(3, k) for k in (-2, -1, 0, 1, 2)] + [(2, k) for k in (-1, 0, 1)] + [(1, 0)]
UPPER = [(0, k) for k in (-1, 0, 1, 2)] + [(1, k) for k in (0, 1)]
LOWER_POT = [(3, -1), (3, 0), (3, 1), (2, 0)]
UPPER_POT = [(0, 0), (0, 1)]
PHASES = (("x", "zlo", "zhi"), ("core", "y"))
POLE = ("x", "zlo", "core")
SLAB = ("y", "zhi")


def own_row():
    return lax.axis_index(POLE)


def gather_rows(row_ref, vectors, potential, own, up, down, levels_out, sems):
    row = row_ref[0]
    copies = [pltpu.make_async_copy(potential, levels_out, sems.at[NZ * len(WIDE)])]
    for z in (3, 0, 2, 1):
        for k in WIDE:
            at = lax.rem(row + (k + NX), NX)
            slot = z * len(WIDE) + k + 2
            copies.append(
                pltpu.make_async_copy(vectors.at[:, :, z, at, :], own.at[slot], sems.at[slot])
            )
    for copy in copies:
        copy.start()
    for copy in copies:
        copy.wait()

    def send(out, cells, levels):
        for i, (z, k) in enumerate(cells):
            block = own[z * len(WIDE) + k + 2]
            out[pl.ds(i * ROWS, ROWS), :] = block.reshape(ROWS, 128)
        for i, (z, k) in enumerate(levels):
            at = lax.rem(row + (k + NX), NX)
            out[pl.ds(len(cells) * ROWS + i, 1), :] = levels_out[z, pl.ds(at, 1), :]
        rest = 8 - len(levels)
        out[pl.ds(len(cells) * ROWS + len(levels), rest), :] = jnp.zeros((rest, 128), jnp.float32)

    send(down, UPPER, UPPER_POT)
    send(up, LOWER, LOWER_POT)


def krylov_gram(row_ref, own, above, below, potential, packed, fields, stack):
    row = row_ref[0]
    v0, diag = {}, {}
    for z in range(NZ):
        for k in WIDE:
            v0[z, k] = own[z * len(WIDE) + k + 2].reshape(ROWS, 128)
        for k in (-1, 0, 1, 2):
            at = lax.rem(row + (k + NX), NX)
            diag[z, k] = potential[z, pl.ds(at, 1), :] + (3.0 - BASE)
    for i, (z, k) in enumerate(UPPER):
        v0[z + NZ, k] = above[pl.ds(i * ROWS, ROWS), :]
    for i, (z, k) in enumerate(UPPER_POT):
        diag[z + NZ, k] = above[pl.ds(len(UPPER) * ROWS + i, 1), :] + (3.0 - BASE)
    for i, (z, k) in enumerate(LOWER):
        v0[z - NZ, k] = below[pl.ds(i * ROWS, ROWS), :]
    for i, (z, k) in enumerate(LOWER_POT):
        diag[z - NZ, k] = below[pl.ds(len(LOWER) * ROWS + i, 1), :] + (3.0 - BASE)

    def apply(v, z, k):
        here = v[z, k]
        beside = v[z - 1, k] + v[z + 1, k] + (v[z, k - 1] + v[z, k + 1])
        beside = beside + (pltpu.roll(here, 1, 1) + pltpu.roll(here, 127, 1))
        return diag[z, k] * here - 0.5 * beside

    v1, v2 = {}, {}
    for z, k in (
        [(z, 0) for z in range(-2, 5)]
        + [(z, 1) for z in range(-1, 5)]
        + [(z, -1) for z in range(-1, 4)]
        + [(z, 2) for z in range(0, 4)]
    ):
        v1[z, k] = apply(v0, z, k)
    for z, k in [(z, 0) for z in range(-1, 4)] + [(z, 1) for z in range(0, 4)]:
        v2[z, k] = apply(v1, z, k)
    for z in range(NZ):
        here = v2[z, 0]
        ahead = v2[z - 1, 0] + v2[z, 1] + pltpu.roll(here, 127, 1)
        half = 0.5 * (diag[z, 0] * here - ahead)
        for i, block in enumerate((v0[z, 0], v1[z, 0], here)):
            fields[z, pl.ds(i * ROWS, ROWS), :] = block
            stack[pl.ds(i * ROWS, ROWS), pl.ds(z * 128, 128)] = block
        stack[pl.ds(3 * ROWS, ROWS), pl.ds(z * 128, 128)] = half
    gram = lax.dot_general(
        stack[...],
        stack[...],
        (((1,), (1,)), ((), ())),
        precision=lax.Precision.HIGHEST,
        preferred_element_type=jnp.float32,
    )
    lane = lax.broadcasted_iota(jnp.int32, (NB, 128), 1)
    sub = lax.broadcasted_iota(jnp.int32, (NB, 128), 0)
    result = jnp.zeros((NB, 128), jnp.float32)
    blocks = [[(0, 0)], [(0, 1)], [(1, 1)], [(1, 2)], [(2, 2)], [(2, 3), (3, 2)]]
    for n, parts in enumerate(blocks):
        rr = ri = ir = ii = 0.0
        for i, j in parts:
            top = gram[ROWS * i : ROWS * i + NB, :]
            low = gram[ROWS * i + NB : ROWS * i + ROWS, :]
            first = (NB * n - ROWS * j) % 128
            second = (NB * n - ROWS * j - NB) % 128
            rr = rr + (pltpu.roll(top, first, 1) if first else top)
            ri = ri + (pltpu.roll(top, second, 1) if second else top)
            ir = ir + (pltpu.roll(low, first, 1) if first else low)
            ii = ii + (pltpu.roll(low, second, 1) if second else low)
        col = lane - NB * n
        inside = (col >= 0) & (col < NB)
        result = jnp.where(inside, jnp.where(col >= sub, rr + ii, ri - ir), result)
        on = col == sub
        m_re = jnp.sum(jnp.where(on, rr - ii, 0.0), axis=1, keepdims=True)
        m_im = jnp.sum(jnp.where(on, ri + ir, 0.0), axis=1, keepdims=True)
        result = jnp.where(lane == 6 * NB + 2 * n, m_re, result)
        result = jnp.where(lane == 6 * NB + 2 * n + 1, m_im, result)
    packed[...] = result


def cmul(a, b):
    return (a[0] * b[0] - a[1] * b[1], a[0] * b[1] + a[1] * b[0])


def cadd(a, b):
    return (a[0] + b[0], a[1] + b[1])


def csub(a, b):
    return (a[0] - b[0], a[1] - b[1])


def cdiv(a, b):
    size = b[0] * b[0] + b[1] * b[1]
    return ((a[0] * b[0] + a[1] * b[1]) / size, (a[1] * b[0] - a[0] * b[1]) / size)


def combine(poles, cells, parts, total, fields, filtered, correlation, energy):
    moments = total[...]
    lane = lax.broadcasted_iota(jnp.int32, (NB, 128), 1)
    m = [
        tuple(
            jnp.broadcast_to(moments[:, 6 * NB + 2 * n + c : 6 * NB + 2 * n + c + 1], (NB, 128))
            for c in (0, 1)
        )
        for n in range(6)
    ]
    cosine = jnp.zeros((NB, 128), jnp.float32)
    sine = jnp.zeros((NB, 128), jnp.float32)
    for j in range(poles):
        angle = 2.0 * math.pi / poles * (j + 0.5)
        cosine = jnp.where(lane == j, math.cos(angle), cosine)
        sine = jnp.where(lane == j, math.sin(angle), sine)
    shift = (contour_center + contour_radius * cosine, contour_radius * sine)
    weight = (contour_radius * cosine / poles, contour_radius * sine / poles)
    zeta = (shift[0] - BASE, shift[1])

    def form(p, q):
        sums = {}
        for i, a in enumerate(p):
            for j, b in enumerate(q):
                ab = cmul(a, b)
                sums[i + j] = cadd(sums[i + j], ab) if i + j in sums else ab
        out = None
        for n, s in sums.items():
            term = cmul(s, m[n])
            out = term if out is None else cadd(out, term)
        return out

    def applied(p):
        q = [cmul(zeta, a) for a in p]
        q = [q[0]] + [csub(q[i], p[i - 1]) for i in range(1, len(p))]
        return q + [(-p[-1][0], -p[-1][1])]

    one = (jnp.ones((NB, 128), jnp.float32), jnp.zeros((NB, 128), jnp.float32))
    residual, direction, solution_ = [one], [one], []
    rho = m[0]
    for iteration in range(3):
        q = applied(direction)
        alpha = cdiv(rho, form(direction, q))
        step = [cmul(alpha, d) for d in direction]
        solution_ = [cadd(s, t) for s, t in zip(solution_, step)] + step[len(solution_) :]
        step = [cmul(alpha, d) for d in q]
        residual = [csub(r, t) for r, t in zip(residual, step)] + [
            (-t[0], -t[1]) for t in step[len(residual) :]
        ]
        if iteration < 2:
            rho_new = form(residual, residual)
            beta = cdiv(rho_new, rho)
            step = [cmul(beta, d) for d in direction]
            direction = [cadd(r, t) for r, t in zip(residual, step)] + residual[len(step) :]
            rho = rho_new
    image = []
    for k in range(4):
        term = residual[k]
        if k < 3:
            term = cadd(term, cmul(shift, solution_[k]))
        if k == 0:
            term = (term[0] - 1.0, term[1])
        image.append(term)

    def over_poles(term):
        term = cmul(weight, term)
        return tuple(
            jnp.sum(jnp.where(lane < poles, t, 0.0), axis=1, keepdims=True) for t in term
        )

    coef = [over_poles(s) for s in solution_]
    coef_image = [over_poles(s) for s in image]
    for z in range(NZ):
        re = im = 0.0
        for k in range(3):
            v_re = fields[z, pl.ds(k * ROWS, NB), :]
            v_im = fields[z, pl.ds(k * ROWS + NB, NB), :]
            re = re + (coef[k][0] * v_re - coef[k][1] * v_im)
            im = im + (coef[k][0] * v_im + coef[k][1] * v_re)
        filtered[0, :, z, :] = re
        filtered[1, :, z, :] = im

    a = lax.broadcasted_iota(jnp.int32, (NB, NB), 0)
    b = lax.broadcasted_iota(jnp.int32, (NB, NB), 1)
    flipped = lax.dot_general(
        moments,
        jnp.where(a == b, 1.0, 0.0),
        (((0,), (0,)), ((), ())),
        precision=lax.Precision.HIGHEST,
        preferred_element_type=jnp.float32,
    )
    inner = []
    for n in range(6):
        here = moments[:, NB * n : NB * n + NB]
        there = flipped[NB * n : NB * n + NB, :]
        inner.append(
            (
                jnp.where(b >= a, here, there),
                jnp.where(b < a, here, jnp.where(b > a, -there, 0.0)),
            )
        )

    def as_row(c):
        return tuple(
            jnp.sum(jnp.where(a == b, jnp.broadcast_to(t, (NB, NB)), 0.0), axis=0, keepdims=True)
            for t in c
        )

    def product(right, out):
        rows = [as_row(c) for c in right]
        result = None
        for k in range(3):
            part = None
            for l, r in enumerate(rows):
                term = cmul(r, inner[k + l])
                part = term if part is None else cadd(part, term)
            term = cmul((coef[k][0], -coef[k][1]), part)
            result = term if result is None else cadd(result, term)
        out[0] = result[0] * (1.0 / cells)
        out[1] = result[1] * (1.0 / cells)

    product(coef, correlation)
    product(coef_image, energy)


def on_device(vectors, potential):
    f32 = jnp.float32
    vmem = pl.BlockSpec(memory_space=pltpu.VMEM)
    smem = pl.BlockSpec(memory_space=pltpu.SMEM)
    vectors = pltpu.with_memory_space_constraint(vectors, pltpu.HBM)
    potential = pltpu.with_memory_space_constraint(potential, pltpu.HBM)
    row = own_row().reshape(1).astype(jnp.int32)
    slots = NZ * len(WIDE)
    own, up, down, levels = pl.pallas_call(
        gather_rows,
        in_specs=[smem] + [pl.BlockSpec(memory_space=pltpu.HBM)] * 2,
        out_specs=[vmem] * 4,
        out_shape=[
            jax.ShapeDtypeStruct((slots, 2, NB, 128), f32),
            jax.ShapeDtypeStruct((len(LOWER) * ROWS + 8, 128), f32),
            jax.ShapeDtypeStruct((len(UPPER) * ROWS + 8, 128), f32),
            jax.ShapeDtypeStruct(potential.shape, f32),
        ],
        scratch_shapes=[pltpu.SemaphoreType.DMA((slots + 1,))],
        name="gather_rows", compiler_params=pltpu.CompilerParams(vmem_limit_bytes=8 << 20),
    )(row, vectors, potential)
    slabs = lax.axis_size(SLAB)
    ahead = [(i, (i + 1) % slabs) for i in range(slabs)]
    back = [(i, (i - 1) % slabs) for i in range(slabs)]
    below = lax.ppermute(up, SLAB, ahead)
    above = lax.ppermute(down, SLAB, back)
    packed, fields = pl.pallas_call(
        krylov_gram,
        in_specs=[smem] + [vmem] * 4,
        out_specs=[vmem] * 2,
        out_shape=[
            jax.ShapeDtypeStruct((NB, 128), f32),
            jax.ShapeDtypeStruct((NZ, 3 * ROWS, 128), f32),
        ],
        scratch_shapes=[pltpu.VMEM((4 * ROWS, NZ * 128), f32)],
        name="krylov_gram", compiler_params=pltpu.CompilerParams(vmem_limit_bytes=8 << 20),
    )(row, own, above, below, levels)
    for axes in PHASES:
        count = lax.axis_size(axes)
        shared = jnp.broadcast_to(packed[None], (count, NB, 128))
        packed = jnp.sum(lax.all_to_all(shared, axes, 0, 0), axis=0)
    cells = NZ * slabs * NX * 128
    filtered, correlation, energy = pl.pallas_call(
        functools.partial(combine, lax.axis_size(POLE), cells, None),
        in_specs=[vmem] * 2,
        out_specs=[vmem] * 3,
        out_shape=[
            jax.ShapeDtypeStruct((2, NB, NZ, 128), f32),
            jax.ShapeDtypeStruct((2, NB, NB), f32),
            jax.ShapeDtypeStruct((2, NB, NB), f32),
        ],
        name="combine", compiler_params=pltpu.CompilerParams(vmem_limit_bytes=8 << 20),
    )(packed, fields)
    return filtered[:, :, :, None, :], correlation, energy


def solution(mesh):
    fine = Mesh(mesh.devices.reshape(4, 2, 2, 8, 4), POLE + SLAB)
    in_specs = (P(None, None, SLAB, None, None), P(SLAB, None, None))
    out_specs = (P(None, None, SLAB, POLE, None), P(), P())
    return jax.shard_map(
        on_device, mesh=fine, in_specs=in_specs, out_specs=out_specs, check_vma=False
    )
```

```python
import functools
import math

import jax
import jax.numpy as jnp
from jax import lax
from jax.experimental import pallas as pl
from jax.experimental.pallas import tpu as pltpu
from jax.sharding import Mesh
from jax.sharding import PartitionSpec as P

contour_center = 2.0
contour_radius = 1.5
BASE = 4.0
NB = 16
ROWS = 2 * NB
NZ = 4
NX = 16
EDGE = {3: (-2, -1, 0, 1, 2), 2: (-1, 0, 1), 1: (0, 1), 0: (-1, 0, 1, 2)}
WIDE = {z: (-2, -1, 0, 1, 2, 3) for z in (0, 1, 2, 3)}
PHASES = (("x", "zlo", "zhi"), ("core", "y"))
POLE = ("x", "zlo", "core")
SLAB = ("y", "zhi")


def own_row():
    return lax.axis_index(POLE)


def fetch(row, vectors, rows, buffer, sems):
    copies, slots = [], {}
    for z in rows:
        for k in rows[z]:
            at = lax.rem(row + (k + NX), NX)
            slot = slots[z, k] = len(slots)
            copies.append(
                pltpu.make_async_copy(vectors.at[:, :, z, at, :], buffer.at[slot], sems.at[slot])
            )
            copies[-1].start()
    return copies, slots


def turned(v):
    return pltpu.roll(v, 1, 1) + pltpu.roll(v, 127, 1)


class Slab:
    def __init__(self, row, levels):
        self.row, self.levels, self.diagonals = row, levels, {}

    def diagonal(self, z, k):
        if (z, k) not in self.diagonals:
            at = lax.rem(self.row + (k + NX), NX)
            self.diagonals[z, k] = self.levels[z, pl.ds(at, 1), :] + (3.0 - BASE)
        return self.diagonals[z, k]

    def apply(self, v, z, k):
        beside = turned(v(z, k)) + (v(z, k - 1) + v(z, k + 1))
        if z > 0:
            beside = beside + v(z - 1, k)
        if z < NZ - 1:
            beside = beside + v(z + 1, k)
        return self.diagonal(z, k) * v(z, k) - 0.5 * beside


def slab_edges(row_ref, vectors, potential, up, down, buffer, levels, sems):
    row = row_ref[0]
    level_copy = pltpu.make_async_copy(potential, levels, sems.at[sum(map(len, EDGE.values()))])
    level_copy.start()
    copies, slots = fetch(row, vectors, EDGE, buffer, sems)
    for copy in [level_copy] + copies:
        copy.wait()
    slab = Slab(row, levels)

    def field(z, k):
        return buffer[slots[z, k]].reshape(ROWS, 128)

    def into_next(z, inner, k):
        around = turned(field(z, k)) + (field(z, k - 1) + field(z, k + 1))
        return 0.5 * (around - slab.diagonal(z, k) * field(z, k)) + 0.25 * field(inner, k)

    first = {}
    for z, k in [(2, 0), (3, -1), (3, 0), (3, 1)]:
        first[z, k] = slab.apply(field, z, k)
    second = slab.apply(lambda z, k: first[z, k], 3, 0) + 0.25 * field(3, 0)
    out = [field(3, 0), field(3, 1), into_next(3, 2, 0), into_next(3, 2, 1), second]
    for i, block in enumerate(out):
        up[pl.ds(i * ROWS, ROWS), :] = block
    up[pl.ds(len(out) * ROWS, 8), :] = jnp.broadcast_to(slab.diagonal(3, 0), (8, 128))
    out = [field(0, 0), field(0, 1), into_next(0, 1, 0), into_next(0, 1, 1)]
    for i, block in enumerate(out):
        down[pl.ds(i * ROWS, ROWS), :] = block


def slab_fields(row_ref, vectors, potential, inside, diagonals, buffer, levels, sems):
    row = row_ref[0]
    level_copy = pltpu.make_async_copy(potential, levels, sems.at[sum(map(len, WIDE.values()))])
    level_copy.start()
    copies, slots = fetch(row, vectors, WIDE, buffer, sems)
    for copy in [level_copy] + copies:
        copy.wait()
    slab = Slab(row, levels)

    def field(z, k):
        return buffer[slots[z, k]].reshape(ROWS, 128)

    first = {}
    for z in range(NZ):
        for k in (-1, 0, 1, 2):
            first[z, k] = slab.apply(field, z, k)
    for z in range(NZ):
        inside[z, 0] = field(z, 0)
        inside[z, 1] = first[z, 0]
        for k in (0, 1):
            second = slab.apply(lambda z, k: first[z, k], z, k)
            if z in (0, NZ - 1):
                second = second + 0.25 * field(z, k)
            inside[z, 2 + k] = second
            diagonals[pl.ds(2 * z + k, 1), :] = slab.diagonal(z, k)


def krylov_gram(inside, diagonals, below, above, down, packed, fields, stack):
    def part(halo, i):
        return halo[pl.ds(i * ROWS, ROWS), :]

    def level(z, k):
        return diagonals[pl.ds(2 * z + k, 1), :]

    v1, v2 = {}, {}
    for z in range(NZ):
        v1[z] = inside[z, 1]
        for k in (0, 1):
            v2[z, k] = inside[z, 2 + k]
    for z, near, halo in [(0, 1, below), (3, 2, above)]:
        v1[z] = v1[z] - 0.5 * part(halo, 0)
        for k in (0, 1):
            v2[z, k] = v2[z, k] + (part(halo, 2 + k) - 0.5 * (level(z, k) * part(halo, k)))
            v2[near, k] = v2[near, k] + 0.25 * part(halo, k)
    lowest = below[pl.ds(5 * ROWS, 1), :]
    v2[-1, 0] = part(below, 4) + (part(down, 2) - 0.5 * (lowest * part(down, 0)))
    for z in range(NZ):
        here = v2[z, 0]
        ahead = v2[z - 1, 0] + v2[z, 1] + pltpu.roll(here, 127, 1)
        half = 0.5 * (level(z, 0) * here - ahead)
        fields[z, 0] = v1[z]
        fields[z, 1] = here
        for i, block in enumerate((inside[z, 0], v1[z], here, half)):
            stack[pl.ds(i * ROWS, ROWS), pl.ds(z * 128, 128)] = block
    gram = lax.dot_general(
        stack[...],
        stack[...],
        (((1,), (1,)), ((), ())),
        precision=lax.Precision.HIGHEST,
        preferred_element_type=jnp.float32,
    )
    lane = lax.broadcasted_iota(jnp.int32, (NB, 128), 1)
    sub = lax.broadcasted_iota(jnp.int32, (NB, 128), 0)
    result = jnp.zeros((NB, 128), jnp.float32)
    blocks = [[(0, 0)], [(0, 1)], [(1, 1)], [(1, 2)], [(2, 2)], [(2, 3), (3, 2)]]
    for n, parts in enumerate(blocks):
        rr = ri = ir = ii = 0.0
        for i, j in parts:
            top = gram[ROWS * i : ROWS * i + NB, :]
            low = gram[ROWS * i + NB : ROWS * i + ROWS, :]
            first = (NB * n - ROWS * j) % 128
            second = (NB * n - ROWS * j - NB) % 128
            rr = rr + (pltpu.roll(top, first, 1) if first else top)
            ri = ri + (pltpu.roll(top, second, 1) if second else top)
            ir = ir + (pltpu.roll(low, first, 1) if first else low)
            ii = ii + (pltpu.roll(low, second, 1) if second else low)
        col = lane - NB * n
        inside = (col >= 0) & (col < NB)
        result = jnp.where(inside, jnp.where(col >= sub, rr + ii, ri - ir), result)
        on = col == sub
        m_re = jnp.sum(jnp.where(on, rr - ii, 0.0), axis=1, keepdims=True)
        m_im = jnp.sum(jnp.where(on, ri + ir, 0.0), axis=1, keepdims=True)
        result = jnp.where(lane == 6 * NB + 2 * n, m_re, result)
        result = jnp.where(lane == 6 * NB + 2 * n + 1, m_im, result)
    packed[...] = result


def cmul(a, b):
    return (a[0] * b[0] - a[1] * b[1], a[0] * b[1] + a[1] * b[0])


def cadd(a, b):
    return (a[0] + b[0], a[1] + b[1])


def csub(a, b):
    return (a[0] - b[0], a[1] - b[1])


def cdiv(a, b):
    size = b[0] * b[0] + b[1] * b[1]
    return ((a[0] * b[0] + a[1] * b[1]) / size, (a[1] * b[0] - a[0] * b[1]) / size)


def combine(poles, cells, total, inside, fields, filtered, correlation, energy):
    moments = total[...]
    lane = lax.broadcasted_iota(jnp.int32, (NB, 128), 1)
    m = [
        tuple(
            jnp.broadcast_to(moments[:, 6 * NB + 2 * n + c : 6 * NB + 2 * n + c + 1], (NB, 128))
            for c in (0, 1)
        )
        for n in range(6)
    ]
    cosine = jnp.zeros((NB, 128), jnp.float32)
    sine = jnp.zeros((NB, 128), jnp.float32)
    for j in range(poles):
        angle = 2.0 * math.pi / poles * (j + 0.5)
        cosine = jnp.where(lane == j, math.cos(angle), cosine)
        sine = jnp.where(lane == j, math.sin(angle), sine)
    shift = (contour_center + contour_radius * cosine, contour_radius * sine)
    weight = (contour_radius * cosine / poles, contour_radius * sine / poles)
    zeta = (shift[0] - BASE, shift[1])

    def form(p, q):
        sums = {}
        for i, a in enumerate(p):
            for j, b in enumerate(q):
                ab = cmul(a, b)
                sums[i + j] = cadd(sums[i + j], ab) if i + j in sums else ab
        out = None
        for n, s in sums.items():
            term = cmul(s, m[n])
            out = term if out is None else cadd(out, term)
        return out

    def applied(p):
        q = [cmul(zeta, a) for a in p]
        q = [q[0]] + [csub(q[i], p[i - 1]) for i in range(1, len(p))]
        return q + [(-p[-1][0], -p[-1][1])]

    one = (jnp.ones((NB, 128), jnp.float32), jnp.zeros((NB, 128), jnp.float32))
    residual, direction, solution_ = [one], [one], []
    rho = m[0]
    for iteration in range(3):
        q = applied(direction)
        alpha = cdiv(rho, form(direction, q))
        step = [cmul(alpha, d) for d in direction]
        solution_ = [cadd(s, t) for s, t in zip(solution_, step)] + step[len(solution_) :]
        step = [cmul(alpha, d) for d in q]
        residual = [csub(r, t) for r, t in zip(residual, step)] + [
            (-t[0], -t[1]) for t in step[len(residual) :]
        ]
        if iteration < 2:
            rho_new = form(residual, residual)
            beta = cdiv(rho_new, rho)
            step = [cmul(beta, d) for d in direction]
            direction = [cadd(r, t) for r, t in zip(residual, step)] + residual[len(step) :]
            rho = rho_new
    image = []
    for k in range(4):
        term = residual[k]
        if k < 3:
            term = cadd(term, cmul(shift, solution_[k]))
        if k == 0:
            term = (term[0] - 1.0, term[1])
        image.append(term)

    def over_poles(term):
        term = cmul(weight, term)
        return tuple(
            jnp.sum(jnp.where(lane < poles, t, 0.0), axis=1, keepdims=True) for t in term
        )

    coef = [over_poles(s) for s in solution_]
    coef_image = [over_poles(s) for s in image]
    for z in range(NZ):
        re = im = 0.0
        for k in range(3):
            v = inside[z, 0] if k == 0 else fields[z, k - 1]
            v_re, v_im = v[:NB], v[NB:]
            re = re + (coef[k][0] * v_re - coef[k][1] * v_im)
            im = im + (coef[k][0] * v_im + coef[k][1] * v_re)
        filtered[0, :, z, :] = re
        filtered[1, :, z, :] = im

    a = lax.broadcasted_iota(jnp.int32, (NB, NB), 0)
    b = lax.broadcasted_iota(jnp.int32, (NB, NB), 1)
    flipped = lax.dot_general(
        moments,
        jnp.where(a == b, 1.0, 0.0),
        (((0,), (0,)), ((), ())),
        precision=lax.Precision.HIGHEST,
        preferred_element_type=jnp.float32,
    )
    inner = []
    for n in range(6):
        here = moments[:, NB * n : NB * n + NB]
        there = flipped[NB * n : NB * n + NB, :]
        inner.append(
            (
                jnp.where(b >= a, here, there),
                jnp.where(b < a, here, jnp.where(b > a, -there, 0.0)),
            )
        )

    def as_row(c):
        return tuple(
            jnp.sum(jnp.where(a == b, jnp.broadcast_to(t, (NB, NB)), 0.0), axis=0, keepdims=True)
            for t in c
        )

    def product(right, out):
        rows = [as_row(c) for c in right]
        result = None
        for k in range(3):
            part = None
            for l, r in enumerate(rows):
                term = cmul(r, inner[k + l])
                part = term if part is None else cadd(part, term)
            term = cmul((coef[k][0], -coef[k][1]), part)
            result = term if result is None else cadd(result, term)
        out[0] = result[0] * (1.0 / cells)
        out[1] = result[1] * (1.0 / cells)

    product(coef, correlation)
    product(coef_image, energy)


def call(kernel, out, scratch, *operands, flops=1 << 20):
    space = {"s": pltpu.SMEM, "h": pltpu.HBM, "v": pltpu.VMEM}
    return pl.pallas_call(
        kernel,
        in_specs=[pl.BlockSpec(memory_space=space[kind]) for kind, _ in operands],
        out_specs=[pl.BlockSpec(memory_space=pltpu.VMEM)] * len(out),
        out_shape=[jax.ShapeDtypeStruct(shape, jnp.float32) for shape in out],
        scratch_shapes=scratch,
        compiler_params=pltpu.CompilerParams(vmem_limit_bytes=8 << 20),
        cost_estimate=pl.CostEstimate(flops=flops, bytes_accessed=1 << 19, transcendentals=0),
        name=getattr(kernel, "__name__", "combine"),
    )(*[operand for _, operand in operands])


def on_device(vectors, potential):
    vectors = pltpu.with_memory_space_constraint(vectors, pltpu.HBM)
    potential = pltpu.with_memory_space_constraint(potential, pltpu.HBM)
    row = own_row().reshape(1).astype(jnp.int32)

    def scratch(rows):
        slots = sum(map(len, rows.values()))
        return [
            pltpu.VMEM((slots, 2, NB, 128), jnp.float32),
            pltpu.VMEM(potential.shape, jnp.float32),
            pltpu.SemaphoreType.DMA((slots + 1,)),
        ]

    source = (("s", row), ("h", vectors), ("h", potential))
    up, down = call(
        slab_edges, [(5 * ROWS + 8, 128), (4 * ROWS, 128)], scratch(EDGE), *source
    )
    slabs = lax.axis_size(SLAB)
    below = lax.ppermute(up, SLAB, [(i, (i + 1) % slabs) for i in range(slabs)])
    above = lax.ppermute(down, SLAB, [(i, (i - 1) % slabs) for i in range(slabs)])
    inside, diagonals = call(
        slab_fields, [(NZ, 4, ROWS, 128), (2 * NZ, 128)], scratch(WIDE), *source
    )
    packed, fields = call(
        krylov_gram,
        [(NB, 128), (NZ, 2, ROWS, 128)],
        [pltpu.VMEM((4 * ROWS, NZ * 128), jnp.float32)],
        *(("v", a) for a in (inside, diagonals, below, above, down)),
    )
    for axes in PHASES:
        count = lax.axis_size(axes)
        shared = jnp.broadcast_to(packed[None], (count, NB, 128))
        packed = jnp.sum(lax.all_to_all(shared, axes, 0, 0), axis=0)
    cells = NZ * slabs * NX * 128
    filtered, correlation, energy = call(
        functools.partial(combine, lax.axis_size(POLE), cells),
        [(2, NB, NZ, 128), (2, NB, NB), (2, NB, NB)],
        [],
        *(("v", a) for a in (packed, inside, fields)),
    )
    return filtered[:, :, :, None, :], correlation, energy


def solution(mesh):
    fine = Mesh(mesh.devices.reshape(4, 2, 2, 8, 4), POLE + SLAB)
    in_specs = (P(None, None, SLAB, None, None), P(SLAB, None, None))
    out_specs = (P(None, None, SLAB, POLE, None), P(), P())
    return jax.shard_map(
        on_device, mesh=fine, in_specs=in_specs, out_specs=out_specs, check_vma=False
    )
```

```python
import functools
import math

import jax
import jax.numpy as jnp
from jax import lax
from jax.experimental import pallas as pl
from jax.experimental.pallas import tpu as pltpu
from jax.sharding import Mesh
from jax.sharding import PartitionSpec as P

contour_center = 2.0
contour_radius = 1.5
BASE = 4.0
NB = 16
ROWS = 2 * NB
NZ = 4
NX = 16
EDGE = {3: (-2, -1, 0, 1, 2), 2: (-1, 0, 1), 1: (0,), 0: (-1, 0, 1)}
WIDE = {z: ((-3,) if z > 1 else ()) + (-2, -1, 0, 1, 2, 3) for z in (0, 1, 2, 3)}
PHASES = (("x", "zlo", "zhi"), ("core", "y"))
POLE = ("x", "zlo", "core")
SLAB = ("y", "zhi")


def own_row():
    return lax.axis_index(POLE)


def fetch(row, vectors, rows, buffer, sems):
    copies, slots = [], {}
    for z in rows:
        for k in rows[z]:
            at = lax.rem(row + (k + NX), NX)
            slot = slots[z, k] = len(slots)
            copies.append(
                pltpu.make_async_copy(vectors.at[:, :, z, at, :], buffer.at[slot], sems.at[slot])
            )
            copies[-1].start()
    return copies, slots


def turned(v):
    return pltpu.roll(v, 1, 1) + pltpu.roll(v, 127, 1)


class Slab:
    def __init__(self, row, levels):
        self.row, self.levels, self.diagonals = row, levels, {}

    def diagonal(self, z, k):
        if (z, k) not in self.diagonals:
            at = lax.rem(self.row + (k + NX), NX)
            self.diagonals[z, k] = self.levels[z, pl.ds(at, 1), :] + (3.0 - BASE)
        return self.diagonals[z, k]

    def apply(self, v, z, k):
        beside = turned(v(z, k)) + (v(z, k - 1) + v(z, k + 1))
        if z > 0:
            beside = beside + v(z - 1, k)
        if z < NZ - 1:
            beside = beside + v(z + 1, k)
        return self.diagonal(z, k) * v(z, k) - 0.5 * beside

    def into_next(self, v, z, inner, k):
        around = turned(v(z, k)) + (v(z, k - 1) + v(z, k + 1))
        return 0.5 * (around - self.diagonal(z, k) * v(z, k)) + 0.25 * v(inner, k)


def slab_edges(row_ref, vectors, potential, up, down, buffer, levels, sems):
    row = row_ref[0]
    level_copy = pltpu.make_async_copy(potential, levels, sems.at[sum(map(len, EDGE.values()))])
    level_copy.start()
    copies, slots = fetch(row, vectors, EDGE, buffer, sems)
    for copy in [level_copy] + copies:
        copy.wait()
    slab = Slab(row, levels)

    def field(z, k):
        return buffer[slots[z, k]].reshape(ROWS, 128)

    first = {}
    for z, k in [(2, 0), (3, -1), (3, 0), (3, 1)]:
        first[z, k] = slab.apply(field, z, k)
    second = slab.apply(lambda z, k: first[z, k], 3, 0) + 0.25 * field(3, 0)
    out = [field(3, 0), field(3, 1)]
    out += [slab.into_next(field, 3, 2, k) for k in (0, 1)] + [second]
    for i, block in enumerate(out):
        up[pl.ds(i * ROWS, ROWS), :] = block
    for k in (0, 1):
        up[pl.ds(len(out) * ROWS + 8 * k, 8), :] = jnp.broadcast_to(slab.diagonal(3, k), (8, 128))
    out = [field(0, 0), slab.into_next(field, 0, 1, 0)]
    for i, block in enumerate(out):
        down[pl.ds(i * ROWS, ROWS), :] = block


def slab_fields(
    row_ref, vectors, potential, inside, beside, diagonals, buffer, levels, sems
):
    row = row_ref[0]
    level_copy = pltpu.make_async_copy(potential, levels, sems.at[sum(map(len, WIDE.values()))])
    level_copy.start()
    copies, slots = fetch(row, vectors, WIDE, buffer, sems)
    for copy in [level_copy] + copies:
        copy.wait()
    slab = Slab(row, levels)

    def field(z, k):
        return buffer[slots[z, k]].reshape(ROWS, 128)

    first = {}
    for z in range(NZ):
        for k in ((-2,) if z > 1 else ()) + (-1, 0, 1, 2):
            first[z, k] = slab.apply(field, z, k)
    for k in (0, 1):
        beside[k] = slab.into_next(field, 0, 1, k)
        beside[2 + k] = 0.25 * field(0, k)
    for z in (2, 3):
        second = slab.apply(lambda z, k: first[z, k], z, -1)
        beside[2 + z] = second + 0.25 * field(z, -1) if z == NZ - 1 else second
    for z in range(NZ):
        inside[z, 0] = field(z, 0)
        inside[z, 1] = first[z, 0]
        for k in (0, 1):
            second = slab.apply(lambda z, k: first[z, k], z, k)
            if z in (0, NZ - 1):
                second = second + 0.25 * field(z, k)
            inside[z, 2 + k] = second
            diagonals[pl.ds(2 * z + k, 1), :] = slab.diagonal(z, k)


def krylov_gram(
    inside, beside, diagonals, below, above, packed, fields, stack, seams
):
    def part(halo, i):
        return halo[pl.ds(i * ROWS, ROWS), :]

    def level(z, k):
        return diagonals[pl.ds(2 * z + k, 1), :]

    v1, v2, add = {}, {}, {}
    for z in range(NZ):
        v1[z] = inside[z, 1]
        for k in (0, 1):
            v2[z, k] = inside[z, 2 + k]
    v1[0] = v1[0] - 0.5 * part(below, 0)
    v1[3] = v1[3] - 0.5 * part(above, 0)
    for k in (0, 1):
        add[0, k] = part(below, 2 + k) - 0.5 * (level(0, k) * part(below, k))
        add[1, k] = 0.25 * part(below, k)
    add[3, 0] = part(above, 1) - 0.5 * (level(3, 0) * part(above, 0))
    add[2, 0] = 0.25 * part(above, 0)
    for at, value in add.items():
        v2[at] = v2[at] + value
    given = []
    for k in (0, 1):
        lowest = below[pl.ds(5 * ROWS + 8 * k, 1), :]
        given.append(beside[k] - 2.0 * (lowest * beside[2 + k]))
    v2[-1, 0] = part(below, 4) + given[0]
    for z in range(NZ):
        here = v2[z, 0]
        ahead = v2[z - 1, 0] + v2[z, 1] + pltpu.roll(here, 127, 1)
        half = 0.5 * (level(z, 0) * here - ahead)
        fields[z, 0] = v1[z]
        fields[z, 1] = here
        for i, block in enumerate((inside[z, 0], v1[z], here, half)):
            stack[pl.ds(i * ROWS, ROWS), pl.ds(z * 128, 128)] = block
    pairs = [(add[2, 0], beside[4]), (add[3, 0], beside[5]), (given[0], given[1])]
    pairs.append((beside[2], beside[3]))
    seams[pl.ds(0, 2 * ROWS), :] = jnp.zeros((2 * ROWS, NZ * 128), jnp.float32)
    for i, (one, other) in enumerate(pairs):
        seams[pl.ds(2 * ROWS, ROWS), pl.ds(i * 128, 128)] = one
        seams[pl.ds(3 * ROWS, ROWS), pl.ds(i * 128, 128)] = -0.5 * other

    def outer(a, b):
        return lax.dot_general(
            a,
            b,
            (((1,), (1,)), ((), ())),
            precision=lax.Precision.HIGHEST,
            preferred_element_type=jnp.float32,
        )

    gram = outer(stack[...], stack[...])
    seam = outer(seams[pl.ds(2 * ROWS, 2 * ROWS), :], seams[...])
    lane = lax.broadcasted_iota(jnp.int32, (NB, 128), 1)
    sub = lax.broadcasted_iota(jnp.int32, (NB, 128), 0)
    result = jnp.zeros((NB, 128), jnp.float32)
    blocks = [[(0, 0)], [(0, 1)], [(1, 1)], [(1, 2)], [(2, 2)], [(2, 3), (3, 2)]]
    for n, parts in enumerate(blocks):
        rr = ri = ir = ii = 0.0
        for i, j in parts:
            top = gram[ROWS * i : ROWS * i + NB, :]
            low = gram[ROWS * i + NB : ROWS * i + ROWS, :]
            if n == 5:
                top = top + seam[ROWS * (i - 2) : ROWS * (i - 2) + NB, :]
                low = low + seam[ROWS * (i - 2) + NB : ROWS * (i - 2) + ROWS, :]
            first = (NB * n - ROWS * j) % 128
            second = (NB * n - ROWS * j - NB) % 128
            rr = rr + (pltpu.roll(top, first, 1) if first else top)
            ri = ri + (pltpu.roll(top, second, 1) if second else top)
            ir = ir + (pltpu.roll(low, first, 1) if first else low)
            ii = ii + (pltpu.roll(low, second, 1) if second else low)
        col = lane - NB * n
        inside = (col >= 0) & (col < NB)
        result = jnp.where(inside, jnp.where(col >= sub, rr + ii, ri - ir), result)
        on = col == sub
        m_re = jnp.sum(jnp.where(on, rr - ii, 0.0), axis=1, keepdims=True)
        m_im = jnp.sum(jnp.where(on, ri + ir, 0.0), axis=1, keepdims=True)
        result = jnp.where(lane == 6 * NB + 2 * n, m_re, result)
        result = jnp.where(lane == 6 * NB + 2 * n + 1, m_im, result)
    packed[...] = result


def cmul(a, b):
    return (a[0] * b[0] - a[1] * b[1], a[0] * b[1] + a[1] * b[0])


def cadd(a, b):
    return (a[0] + b[0], a[1] + b[1])


def csub(a, b):
    return (a[0] - b[0], a[1] - b[1])


def cdiv(a, b):
    size = b[0] * b[0] + b[1] * b[1]
    return ((a[0] * b[0] + a[1] * b[1]) / size, (a[1] * b[0] - a[0] * b[1]) / size)


def combine(poles, cells, total, inside, fields, filtered, correlation, energy):
    moments = total[...]
    lane = lax.broadcasted_iota(jnp.int32, (NB, 128), 1)
    m = [
        tuple(
            jnp.broadcast_to(moments[:, 6 * NB + 2 * n + c : 6 * NB + 2 * n + c + 1], (NB, 128))
            for c in (0, 1)
        )
        for n in range(6)
    ]
    cosine = jnp.zeros((NB, 128), jnp.float32)
    sine = jnp.zeros((NB, 128), jnp.float32)
    for j in range(poles):
        angle = 2.0 * math.pi / poles * (j + 0.5)
        cosine = jnp.where(lane == j, math.cos(angle), cosine)
        sine = jnp.where(lane == j, math.sin(angle), sine)
    shift = (contour_center + contour_radius * cosine, contour_radius * sine)
    weight = (contour_radius * cosine / poles, contour_radius * sine / poles)
    zeta = (shift[0] - BASE, shift[1])

    def form(p, q):
        sums = {}
        for i, a in enumerate(p):
            for j, b in enumerate(q):
                ab = cmul(a, b)
                sums[i + j] = cadd(sums[i + j], ab) if i + j in sums else ab
        out = None
        for n, s in sums.items():
            term = cmul(s, m[n])
            out = term if out is None else cadd(out, term)
        return out

    def applied(p):
        q = [cmul(zeta, a) for a in p]
        q = [q[0]] + [csub(q[i], p[i - 1]) for i in range(1, len(p))]
        return q + [(-p[-1][0], -p[-1][1])]

    one = (jnp.ones((NB, 128), jnp.float32), jnp.zeros((NB, 128), jnp.float32))
    residual, direction, solution_ = [one], [one], []
    rho = m[0]
    for iteration in range(3):
        q = applied(direction)
        alpha = cdiv(rho, form(direction, q))
        step = [cmul(alpha, d) for d in direction]
        solution_ = [cadd(s, t) for s, t in zip(solution_, step)] + step[len(solution_) :]
        step = [cmul(alpha, d) for d in q]
        residual = [csub(r, t) for r, t in zip(residual, step)] + [
            (-t[0], -t[1]) for t in step[len(residual) :]
        ]
        if iteration < 2:
            rho_new = form(residual, residual)
            beta = cdiv(rho_new, rho)
            step = [cmul(beta, d) for d in direction]
            direction = [cadd(r, t) for r, t in zip(residual, step)] + residual[len(step) :]
            rho = rho_new
    image = []
    for k in range(4):
        term = residual[k]
        if k < 3:
            term = cadd(term, cmul(shift, solution_[k]))
        if k == 0:
            term = (term[0] - 1.0, term[1])
        image.append(term)

    def over_poles(term):
        term = cmul(weight, term)
        return tuple(
            jnp.sum(jnp.where(lane < poles, t, 0.0), axis=1, keepdims=True) for t in term
        )

    coef = [over_poles(s) for s in solution_]
    coef_image = [over_poles(s) for s in image]
    for z in range(NZ):
        re = im = 0.0
        for k in range(3):
            v = inside[z, 0] if k == 0 else fields[z, k - 1]
            v_re, v_im = v[:NB], v[NB:]
            re = re + (coef[k][0] * v_re - coef[k][1] * v_im)
            im = im + (coef[k][0] * v_im + coef[k][1] * v_re)
        filtered[0, :, z, :] = re
        filtered[1, :, z, :] = im

    a = lax.broadcasted_iota(jnp.int32, (NB, NB), 0)
    b = lax.broadcasted_iota(jnp.int32, (NB, NB), 1)
    flipped = lax.dot_general(
        moments,
        jnp.where(a == b, 1.0, 0.0),
        (((0,), (0,)), ((), ())),
        precision=lax.Precision.HIGHEST,
        preferred_element_type=jnp.float32,
    )
    inner = []
    for n in range(6):
        here = moments[:, NB * n : NB * n + NB]
        there = flipped[NB * n : NB * n + NB, :]
        inner.append(
            (
                jnp.where(b >= a, here, there),
                jnp.where(b < a, here, jnp.where(b > a, -there, 0.0)),
            )
        )

    def as_row(c):
        return tuple(
            jnp.sum(jnp.where(a == b, jnp.broadcast_to(t, (NB, NB)), 0.0), axis=0, keepdims=True)
            for t in c
        )

    def product(right, out):
        rows = [as_row(c) for c in right]
        result = None
        for k in range(3):
            part = None
            for l, r in enumerate(rows):
                term = cmul(r, inner[k + l])
                part = term if part is None else cadd(part, term)
            term = cmul((coef[k][0], -coef[k][1]), part)
            result = term if result is None else cadd(result, term)
        out[0] = result[0] * (1.0 / cells)
        out[1] = result[1] * (1.0 / cells)

    product(coef, correlation)
    product(coef_image, energy)


def call(kernel, out, scratch, *operands, flops=1 << 20):
    space = {"s": pltpu.SMEM, "h": pltpu.HBM, "v": pltpu.VMEM}
    return pl.pallas_call(
        kernel,
        in_specs=[pl.BlockSpec(memory_space=space[kind]) for kind, _ in operands],
        out_specs=[pl.BlockSpec(memory_space=pltpu.VMEM)] * len(out),
        out_shape=[jax.ShapeDtypeStruct(shape, jnp.float32) for shape in out],
        scratch_shapes=scratch,
        compiler_params=pltpu.CompilerParams(vmem_limit_bytes=8 << 20),
        cost_estimate=pl.CostEstimate(flops=flops, bytes_accessed=1 << 19, transcendentals=0),
        name=getattr(kernel, "__name__", "combine"),
    )(*[operand for _, operand in operands])


def on_device(vectors, potential):
    vectors = pltpu.with_memory_space_constraint(vectors, pltpu.HBM)
    potential = pltpu.with_memory_space_constraint(potential, pltpu.HBM)
    row = own_row().reshape(1).astype(jnp.int32)

    def scratch(rows):
        slots = sum(map(len, rows.values()))
        return [
            pltpu.VMEM((slots, 2, NB, 128), jnp.float32),
            pltpu.VMEM(potential.shape, jnp.float32),
            pltpu.SemaphoreType.DMA((slots + 1,)),
        ]

    source = (("s", row), ("h", vectors), ("h", potential))
    up, down = call(
        slab_edges, [(5 * ROWS + 16, 128), (2 * ROWS, 128)], scratch(EDGE), *source
    )
    slabs = lax.axis_size(SLAB)
    below = lax.ppermute(up, SLAB, [(i, (i + 1) % slabs) for i in range(slabs)])
    above = lax.ppermute(down, SLAB, [(i, (i - 1) % slabs) for i in range(slabs)])
    inside, beside, diagonals = call(
        slab_fields,
        [(NZ, 4, ROWS, 128), (6, ROWS, 128), (2 * NZ, 128)],
        scratch(WIDE),
        *source,
    )
    packed, fields = call(
        krylov_gram,
        [(NB, 128), (NZ, 2, ROWS, 128)],
        [pltpu.VMEM((4 * ROWS, NZ * 128), jnp.float32)] * 2,
        *(("v", a) for a in (inside, beside, diagonals, below, above)),
    )
    for axes in PHASES:
        count = lax.axis_size(axes)
        shared = jnp.broadcast_to(packed[None], (count, NB, 128))
        packed = jnp.sum(lax.all_to_all(shared, axes, 0, 0), axis=0)
    cells = NZ * slabs * NX * 128
    filtered, correlation, energy = call(
        functools.partial(combine, lax.axis_size(POLE), cells),
        [(2, NB, NZ, 128), (2, NB, NB), (2, NB, NB)],
        [],
        *(("v", a) for a in (packed, inside, fields)),
    )
    return filtered[:, :, :, None, :], correlation, energy


def solution(mesh):
    fine = Mesh(mesh.devices.reshape(4, 2, 2, 8, 4), POLE + SLAB)
    in_specs = (P(None, None, SLAB, None, None), P(SLAB, None, None))
    out_specs = (P(None, None, SLAB, POLE, None), P(), P())
    return jax.shard_map(
        on_device, mesh=fine, in_specs=in_specs, out_specs=out_specs, check_vma=False
    )
```

```python
import functools
import math

import jax
import jax.numpy as jnp
from jax import lax
from jax.experimental import pallas as pl
from jax.experimental.pallas import tpu as pltpu
from jax.sharding import Mesh
from jax.sharding import PartitionSpec as P

contour_center = 2.0
contour_radius = 1.5
BASE = 4.0
NB = 16
ROWS = 2 * NB
NZ = 4
NX = 16
EDGE = {3: (-2, -1, 0, 1, 2), 2: (-1, 0, 1), 1: (0,), 0: (-1, 0, 1)}
WIDE = {z: ((-3,) if z > 1 else ()) + (-2, -1, 0, 1, 2, 3) for z in (0, 1, 2, 3)}
PHASES = (("x", "zlo", "zhi"), ("core", "y"))
POLE = ("x", "zlo", "core")
SLAB = ("y", "zhi")


def own_row():
    return lax.axis_index(POLE)


def fetch(row, vectors, rows, buffer, sems):
    copies, slots = [], {}
    for z in rows:
        for k in rows[z]:
            at = lax.rem(row + (k + NX), NX)
            slot = slots[z, k] = len(slots)
            copies.append(
                pltpu.make_async_copy(vectors.at[:, :, z, at, :], buffer.at[slot], sems.at[slot])
            )
            copies[-1].start()
    return copies, slots


def turned(v):
    return pltpu.roll(v, 1, 1) + pltpu.roll(v, 127, 1)


class Slab:
    def __init__(self, row, levels):
        self.row, self.levels, self.diagonals = row, levels, {}

    def diagonal(self, z, k):
        if (z, k) not in self.diagonals:
            at = lax.rem(self.row + (k + NX), NX)
            self.diagonals[z, k] = self.levels[z, pl.ds(at, 1), :] + (3.0 - BASE)
        return self.diagonals[z, k]

    def apply(self, v, z, k):
        beside = turned(v(z, k)) + (v(z, k - 1) + v(z, k + 1))
        if z > 0:
            beside = beside + v(z - 1, k)
        if z < NZ - 1:
            beside = beside + v(z + 1, k)
        return self.diagonal(z, k) * v(z, k) - 0.5 * beside

    def into_next(self, v, z, inner, k):
        around = turned(v(z, k)) + (v(z, k - 1) + v(z, k + 1))
        return 0.5 * (around - self.diagonal(z, k) * v(z, k)) + 0.25 * v(inner, k)


def slab_edges(row_ref, vectors, potential, up, down, buffer, levels, sems):
    row = row_ref[0]
    level_copy = pltpu.make_async_copy(potential, levels, sems.at[sum(map(len, EDGE.values()))])
    level_copy.start()
    copies, slots = fetch(row, vectors, EDGE, buffer, sems)
    for copy in [level_copy] + copies:
        copy.wait()
    slab = Slab(row, levels)

    def field(z, k):
        return buffer[slots[z, k]].reshape(ROWS, 128)

    first = {}
    for z, k in [(2, 0), (3, -1), (3, 0), (3, 1)]:
        first[z, k] = slab.apply(field, z, k)
    second = slab.apply(lambda z, k: first[z, k], 3, 0) + 0.25 * field(3, 0)
    out = [field(3, 0), field(3, 1)]
    out += [slab.into_next(field, 3, 2, k) for k in (0, 1)] + [second]
    for i, block in enumerate(out):
        up[pl.ds(i * ROWS, ROWS), :] = block
    for k in (0, 1):
        up[pl.ds(len(out) * ROWS + 8 * k, 8), :] = jnp.broadcast_to(slab.diagonal(3, k), (8, 128))
    out = [field(0, 0), slab.into_next(field, 0, 1, 0)]
    for i, block in enumerate(out):
        down[pl.ds(i * ROWS, ROWS), :] = block


def slab_fields(
    row_ref, vectors, potential, inside, beside, diagonals, buffer, levels, sems
):
    row = row_ref[0]
    level_copy = pltpu.make_async_copy(potential, levels, sems.at[sum(map(len, WIDE.values()))])
    level_copy.start()
    copies, slots = fetch(row, vectors, WIDE, buffer, sems)
    for copy in [level_copy] + copies:
        copy.wait()
    slab = Slab(row, levels)

    def field(z, k):
        return buffer[slots[z, k]].reshape(ROWS, 128)

    first = {}
    for z in range(NZ):
        for k in ((-2,) if z > 1 else ()) + (-1, 0, 1, 2):
            first[z, k] = slab.apply(field, z, k)
    for k in (0, 1):
        beside[k] = slab.into_next(field, 0, 1, k)
        beside[2 + k] = 0.25 * field(0, k)
    for z in (2, 3):
        second = slab.apply(lambda z, k: first[z, k], z, -1)
        beside[2 + z] = second + 0.25 * field(z, -1) if z == NZ - 1 else second
    for z in range(NZ):
        inside[z, 0] = field(z, 0)
        inside[z, 1] = first[z, 0]
        for k in (0, 1):
            second = slab.apply(lambda z, k: first[z, k], z, k)
            if z in (0, NZ - 1):
                second = second + 0.25 * field(z, k)
            inside[z, 2 + k] = second
            diagonals[pl.ds(2 * z + k, 1), :] = slab.diagonal(z, k)


def krylov_gram(
    inside, beside, diagonals, below, above, packed, fields, stack, seams
):
    def part(halo, i):
        return halo[pl.ds(i * ROWS, ROWS), :]

    def level(z, k):
        return diagonals[pl.ds(2 * z + k, 1), :]

    v1, v2, add = {}, {}, {}
    for z in range(NZ):
        v1[z] = inside[z, 1]
        for k in (0, 1):
            v2[z, k] = inside[z, 2 + k]
    v1[0] = v1[0] - 0.5 * part(below, 0)
    v1[3] = v1[3] - 0.5 * part(above, 0)
    for k in (0, 1):
        add[0, k] = part(below, 2 + k) - 0.5 * (level(0, k) * part(below, k))
        add[1, k] = 0.25 * part(below, k)
    add[3, 0] = part(above, 1) - 0.5 * (level(3, 0) * part(above, 0))
    add[2, 0] = 0.25 * part(above, 0)
    for at, value in add.items():
        v2[at] = v2[at] + value
    given = []
    for k in (0, 1):
        lowest = below[pl.ds(5 * ROWS + 8 * k, 1), :]
        given.append(beside[k] - 2.0 * (lowest * beside[2 + k]))
    v2[-1, 0] = part(below, 4) + given[0]
    for z in range(NZ):
        here = v2[z, 0]
        ahead = v2[z - 1, 0] + v2[z, 1] + pltpu.roll(here, 127, 1)
        half = 0.5 * (level(z, 0) * here - ahead)
        fields[z, 0] = v1[z]
        fields[z, 1] = here
        for i, block in enumerate((inside[z, 0], v1[z], here, half)):
            stack[pl.ds(i * ROWS, ROWS), pl.ds(z * 128, 128)] = block
    pairs = [(add[2, 0], beside[4]), (add[3, 0], beside[5]), (given[0], given[1])]
    pairs.append((beside[2], beside[3]))
    for i, (one, other) in enumerate(pairs):
        seams[pl.ds(0, ROWS), pl.ds(i * 128, 128)] = one
        seams[pl.ds(ROWS, ROWS), pl.ds(i * 128, 128)] = -0.5 * other

    def outer(a, b):
        return lax.dot_general(
            a,
            b,
            (((1,), (1,)), ((), ())),
            precision=lax.Precision.HIGHEST,
            preferred_element_type=jnp.float32,
        )

    gram = outer(stack[...], stack[...])
    seam = outer(seams[...], seams[...])
    seam = jnp.concatenate([jnp.zeros((2 * ROWS, 2 * ROWS), jnp.float32), seam], axis=1)
    lane = lax.broadcasted_iota(jnp.int32, (NB, 128), 1)
    sub = lax.broadcasted_iota(jnp.int32, (NB, 128), 0)
    result = jnp.zeros((NB, 128), jnp.float32)
    blocks = [[(0, 0)], [(0, 1)], [(1, 1)], [(1, 2)], [(2, 2)], [(2, 3), (3, 2)]]
    for n, parts in enumerate(blocks):
        rr = ri = ir = ii = 0.0
        for i, j in parts:
            top = gram[ROWS * i : ROWS * i + NB, :]
            low = gram[ROWS * i + NB : ROWS * i + ROWS, :]
            if n == 5:
                top = top + seam[ROWS * (i - 2) : ROWS * (i - 2) + NB, :]
                low = low + seam[ROWS * (i - 2) + NB : ROWS * (i - 2) + ROWS, :]
            first = (NB * n - ROWS * j) % 128
            second = (NB * n - ROWS * j - NB) % 128
            rr = rr + (pltpu.roll(top, first, 1) if first else top)
            ri = ri + (pltpu.roll(top, second, 1) if second else top)
            ir = ir + (pltpu.roll(low, first, 1) if first else low)
            ii = ii + (pltpu.roll(low, second, 1) if second else low)
        col = lane - NB * n
        inside = (col >= 0) & (col < NB)
        result = jnp.where(inside, jnp.where(col >= sub, rr + ii, ri - ir), result)
        on = col == sub
        m_re = jnp.sum(jnp.where(on, rr - ii, 0.0), axis=1, keepdims=True)
        m_im = jnp.sum(jnp.where(on, ri + ir, 0.0), axis=1, keepdims=True)
        result = jnp.where(lane == 6 * NB + 2 * n, m_re, result)
        result = jnp.where(lane == 6 * NB + 2 * n + 1, m_im, result)
    packed[...] = result


def cmul(a, b):
    return (a[0] * b[0] - a[1] * b[1], a[0] * b[1] + a[1] * b[0])


def cadd(a, b):
    return (a[0] + b[0], a[1] + b[1])


def csub(a, b):
    return (a[0] - b[0], a[1] - b[1])


def cdiv(a, b):
    size = b[0] * b[0] + b[1] * b[1]
    return ((a[0] * b[0] + a[1] * b[1]) / size, (a[1] * b[0] - a[0] * b[1]) / size)


def combine(poles, cells, total, inside, fields, filtered, correlation, energy):
    moments = total[...]
    lane = lax.broadcasted_iota(jnp.int32, (NB, 128), 1)
    m = [
        tuple(
            jnp.broadcast_to(moments[:, 6 * NB + 2 * n + c : 6 * NB + 2 * n + c + 1], (NB, 128))
            for c in (0, 1)
        )
        for n in range(6)
    ]
    cosine = jnp.zeros((NB, 128), jnp.float32)
    sine = jnp.zeros((NB, 128), jnp.float32)
    for j in range(poles):
        angle = 2.0 * math.pi / poles * (j + 0.5)
        cosine = jnp.where(lane == j, math.cos(angle), cosine)
        sine = jnp.where(lane == j, math.sin(angle), sine)
    shift = (contour_center + contour_radius * cosine, contour_radius * sine)
    weight = (contour_radius * cosine / poles, contour_radius * sine / poles)
    zeta = (shift[0] - BASE, shift[1])

    def form(p, q):
        sums = {}
        for i, a in enumerate(p):
            for j, b in enumerate(q):
                ab = cmul(a, b)
                sums[i + j] = cadd(sums[i + j], ab) if i + j in sums else ab
        out = None
        for n, s in sums.items():
            term = cmul(s, m[n])
            out = term if out is None else cadd(out, term)
        return out

    def applied(p):
        q = [cmul(zeta, a) for a in p]
        q = [q[0]] + [csub(q[i], p[i - 1]) for i in range(1, len(p))]
        return q + [(-p[-1][0], -p[-1][1])]

    one = (jnp.ones((NB, 128), jnp.float32), jnp.zeros((NB, 128), jnp.float32))
    residual, direction, solution_ = [one], [one], []
    rho = m[0]
    for iteration in range(3):
        q = applied(direction)
        alpha = cdiv(rho, form(direction, q))
        step = [cmul(alpha, d) for d in direction]
        solution_ = [cadd(s, t) for s, t in zip(solution_, step)] + step[len(solution_) :]
        step = [cmul(alpha, d) for d in q]
        residual = [csub(r, t) for r, t in zip(residual, step)] + [
            (-t[0], -t[1]) for t in step[len(residual) :]
        ]
        if iteration < 2:
            rho_new = form(residual, residual)
            beta = cdiv(rho_new, rho)
            step = [cmul(beta, d) for d in direction]
            direction = [cadd(r, t) for r, t in zip(residual, step)] + residual[len(step) :]
            rho = rho_new
    image = []
    for k in range(4):
        term = residual[k]
        if k < 3:
            term = cadd(term, cmul(shift, solution_[k]))
        if k == 0:
            term = (term[0] - 1.0, term[1])
        image.append(term)

    def over_poles(term):
        term = cmul(weight, term)
        return tuple(
            jnp.sum(jnp.where(lane < poles, t, 0.0), axis=1, keepdims=True) for t in term
        )

    coef = [over_poles(s) for s in solution_]
    coef_image = [over_poles(s) for s in image]
    for z in range(NZ):
        re = im = 0.0
        for k in range(3):
            v = inside[z, 0] if k == 0 else fields[z, k - 1]
            v_re, v_im = v[:NB], v[NB:]
            re = re + (coef[k][0] * v_re - coef[k][1] * v_im)
            im = im + (coef[k][0] * v_im + coef[k][1] * v_re)
        filtered[0, :, z, :] = re
        filtered[1, :, z, :] = im

    a = lax.broadcasted_iota(jnp.int32, (NB, NB), 0)
    b = lax.broadcasted_iota(jnp.int32, (NB, NB), 1)
    flipped = lax.dot_general(
        moments,
        jnp.where(a == b, 1.0, 0.0),
        (((0,), (0,)), ((), ())),
        precision=lax.Precision.HIGHEST,
        preferred_element_type=jnp.float32,
    )
    inner = []
    for n in range(6):
        here = moments[:, NB * n : NB * n + NB]
        there = flipped[NB * n : NB * n + NB, :]
        inner.append(
            (
                jnp.where(b >= a, here, there),
                jnp.where(b < a, here, jnp.where(b > a, -there, 0.0)),
            )
        )

    def as_row(c):
        return tuple(
            jnp.sum(jnp.where(a == b, jnp.broadcast_to(t, (NB, NB)), 0.0), axis=0, keepdims=True)
            for t in c
        )

    def product(right, out):
        rows = [as_row(c) for c in right]
        result = None
        for k in range(3):
            part = None
            for l, r in enumerate(rows):
                term = cmul(r, inner[k + l])
                part = term if part is None else cadd(part, term)
            term = cmul((coef[k][0], -coef[k][1]), part)
            result = term if result is None else cadd(result, term)
        out[0] = result[0] * (1.0 / cells)
        out[1] = result[1] * (1.0 / cells)

    product(coef, correlation)
    product(coef_image, energy)


def call(kernel, out, scratch, *operands, flops=1 << 20):
    space = {"s": pltpu.SMEM, "h": pltpu.HBM, "v": pltpu.VMEM}
    return pl.pallas_call(
        kernel,
        in_specs=[pl.BlockSpec(memory_space=space[kind]) for kind, _ in operands],
        out_specs=[pl.BlockSpec(memory_space=pltpu.VMEM)] * len(out),
        out_shape=[jax.ShapeDtypeStruct(shape, jnp.float32) for shape in out],
        scratch_shapes=scratch,
        compiler_params=pltpu.CompilerParams(vmem_limit_bytes=8 << 20),
        cost_estimate=pl.CostEstimate(flops=flops, bytes_accessed=1 << 19, transcendentals=0),
        name=getattr(kernel, "__name__", "combine"),
    )(*[operand for _, operand in operands])


def on_device(vectors, potential):
    vectors = pltpu.with_memory_space_constraint(vectors, pltpu.HBM)
    potential = pltpu.with_memory_space_constraint(potential, pltpu.HBM)
    row = own_row().reshape(1).astype(jnp.int32)

    def scratch(rows):
        slots = sum(map(len, rows.values()))
        return [
            pltpu.VMEM((slots, 2, NB, 128), jnp.float32),
            pltpu.VMEM(potential.shape, jnp.float32),
            pltpu.SemaphoreType.DMA((slots + 1,)),
        ]

    source = (("s", row), ("h", vectors), ("h", potential))
    up, down = call(
        slab_edges, [(5 * ROWS + 16, 128), (2 * ROWS, 128)], scratch(EDGE), *source
    )
    slabs = lax.axis_size(SLAB)
    below = lax.ppermute(up, SLAB, [(i, (i + 1) % slabs) for i in range(slabs)])
    above = lax.ppermute(down, SLAB, [(i, (i - 1) % slabs) for i in range(slabs)])
    inside, beside, diagonals = call(
        slab_fields,
        [(NZ, 4, ROWS, 128), (6, ROWS, 128), (2 * NZ, 128)],
        scratch(WIDE),
        *source,
    )
    packed, fields = call(
        krylov_gram,
        [(NB, 128), (NZ, 2, ROWS, 128)],
        [pltpu.VMEM((rows * ROWS, NZ * 128), jnp.float32) for rows in (4, 2)],
        *(("v", a) for a in (inside, beside, diagonals, below, above)),
    )
    for axes in PHASES:
        count = lax.axis_size(axes)
        shared = jnp.broadcast_to(packed[None], (count, NB, 128))
        packed = jnp.sum(lax.all_to_all(shared, axes, 0, 0), axis=0)
    cells = NZ * slabs * NX * 128
    filtered, correlation, energy = call(
        functools.partial(combine, lax.axis_size(POLE), cells),
        [(2, NB, NZ, 128), (2, NB, NB), (2, NB, NB)],
        [],
        *(("v", a) for a in (packed, inside, fields)),
    )
    return filtered[:, :, :, None, :], correlation, energy


def solution(mesh):
    fine = Mesh(mesh.devices.reshape(4, 2, 2, 8, 4), POLE + SLAB)
    in_specs = (P(None, None, SLAB, None, None), P(SLAB, None, None))
    out_specs = (P(None, None, SLAB, POLE, None), P(), P())
    return jax.shard_map(
        on_device, mesh=fine, in_specs=in_specs, out_specs=out_specs, check_vma=False
    )
```

```python
import functools
import math

import jax
import jax.numpy as jnp
from jax import lax
from jax.experimental import pallas as pl
from jax.experimental.pallas import tpu as pltpu
from jax.sharding import Mesh
from jax.sharding import PartitionSpec as P

contour_center = 2.0
contour_radius = 1.5
BASE = 4.0
NB = 16
ROWS = 2 * NB
NZ = 4
NX = 16
EDGE = {3: (-2, -1, 0, 1, 2), 2: (-1, 0, 1), 1: (0,), 0: (-1, 0, 1)}
WIDE = {z: ((-3,) if z > 1 else ()) + (-2, -1, 0, 1, 2, 3) for z in (0, 1, 2, 3)}
PHASES = (("x", "zlo", "zhi"), ("core", "y"))
POLE = ("x", "zlo", "core")
SLAB = ("y", "zhi")


def own_row():
    return lax.axis_index(POLE)


def fetch(row, vectors, rows, buffer, sems):
    copies, slots = [], {}
    for z in rows:
        for k in rows[z]:
            at = lax.rem(row + (k + NX), NX)
            slot = slots[z, k] = len(slots)
            copies.append(
                pltpu.make_async_copy(vectors.at[:, :, z, at, :], buffer.at[slot], sems.at[slot])
            )
            copies[-1].start()
    return copies, slots


def turned(v):
    return pltpu.roll(v, 1, 1) + pltpu.roll(v, 127, 1)


class Slab:
    def __init__(self, row, levels):
        self.row, self.levels, self.diagonals = row, levels, {}

    def diagonal(self, z, k):
        if (z, k) not in self.diagonals:
            at = lax.rem(self.row + (k + NX), NX)
            self.diagonals[z, k] = self.levels[z, pl.ds(at, 1), :] + (3.0 - BASE)
        return self.diagonals[z, k]

    def apply(self, v, z, k):
        beside = turned(v(z, k)) + (v(z, k - 1) + v(z, k + 1))
        if z > 0:
            beside = beside + v(z - 1, k)
        if z < NZ - 1:
            beside = beside + v(z + 1, k)
        return self.diagonal(z, k) * v(z, k) - 0.5 * beside

    def into_next(self, v, z, inner, k):
        around = turned(v(z, k)) + (v(z, k - 1) + v(z, k + 1))
        return 0.5 * (around - self.diagonal(z, k) * v(z, k)) + 0.25 * v(inner, k)


def slab_edges(row_ref, vectors, potential, up, down, buffer, levels, sems):
    row = row_ref[0]
    level_copy = pltpu.make_async_copy(potential, levels, sems.at[sum(map(len, EDGE.values()))])
    level_copy.start()
    copies, slots = fetch(row, vectors, EDGE, buffer, sems)
    for copy in [level_copy] + copies:
        copy.wait()
    slab = Slab(row, levels)

    def field(z, k):
        return buffer[slots[z, k]].reshape(ROWS, 128)

    first = {}
    for z, k in [(2, 0), (3, -1), (3, 0), (3, 1)]:
        first[z, k] = slab.apply(field, z, k)
    second = slab.apply(lambda z, k: first[z, k], 3, 0) + 0.25 * field(3, 0)
    out = [field(3, 0), field(3, 1)]
    out += [slab.into_next(field, 3, 2, k) for k in (0, 1)] + [second]
    for i, block in enumerate(out):
        up[pl.ds(i * ROWS, ROWS), :] = block
    for k in (0, 1):
        up[pl.ds(len(out) * ROWS + 8 * k, 8), :] = jnp.broadcast_to(slab.diagonal(3, k), (8, 128))
    out = [field(0, 0), slab.into_next(field, 0, 1, 0)]
    for i, block in enumerate(out):
        down[pl.ds(i * ROWS, ROWS), :] = block


def slab_fields(
    row_ref, vectors, potential, inside, beside, diagonals, buffer, levels, sems
):
    row = row_ref[0]
    level_copy = pltpu.make_async_copy(potential, levels, sems.at[sum(map(len, WIDE.values()))])
    level_copy.start()
    copies, slots = fetch(row, vectors, WIDE, buffer, sems)
    for copy in [level_copy] + copies:
        copy.wait()
    slab = Slab(row, levels)

    def field(z, k):
        return buffer[slots[z, k]].reshape(ROWS, 128)

    first = {}
    for z in range(NZ):
        for k in ((-2,) if z > 1 else ()) + (-1, 0, 1, 2):
            first[z, k] = slab.apply(field, z, k)
    for k in (0, 1):
        beside[k] = slab.into_next(field, 0, 1, k)
        beside[2 + k] = 0.25 * field(0, k)
    for z in (2, 3):
        second = slab.apply(lambda z, k: first[z, k], z, -1)
        beside[2 + z] = second + 0.25 * field(z, -1) if z == NZ - 1 else second
    for z in range(NZ):
        inside[z, 0] = field(z, 0)
        inside[z, 1] = first[z, 0]
        for k in (0, 1):
            second = slab.apply(lambda z, k: first[z, k], z, k)
            if z in (0, NZ - 1):
                second = second + 0.25 * field(z, k)
            inside[z, 2 + k] = second
            diagonals[pl.ds(2 * z + k, 1), :] = slab.diagonal(z, k)


def krylov_gram(
    inside, beside, diagonals, below, above, packed, fields, stack, seams
):
    def part(halo, i):
        return halo[pl.ds(i * ROWS, ROWS), :]

    def level(z, k):
        return diagonals[pl.ds(2 * z + k, 1), :]

    v1, v2, add = {}, {}, {}
    for z in range(NZ):
        v1[z] = inside[z, 1]
        for k in (0, 1):
            v2[z, k] = inside[z, 2 + k]
    v1[0] = v1[0] - 0.5 * part(below, 0)
    v1[3] = v1[3] - 0.5 * part(above, 0)
    for k in (0, 1):
        add[0, k] = part(below, 2 + k) - 0.5 * (level(0, k) * part(below, k))
        add[1, k] = 0.25 * part(below, k)
    add[3, 0] = part(above, 1) - 0.5 * (level(3, 0) * part(above, 0))
    add[2, 0] = 0.25 * part(above, 0)
    for at, value in add.items():
        v2[at] = v2[at] + value
    given = []
    for k in (0, 1):
        lowest = below[pl.ds(5 * ROWS + 8 * k, 1), :]
        given.append(beside[k] - 2.0 * (lowest * beside[2 + k]))
    v2[-1, 0] = part(below, 4) + given[0]
    for z in range(NZ):
        here = v2[z, 0]
        ahead = v2[z - 1, 0] + v2[z, 1] + pltpu.roll(here, 127, 1)
        half = 0.5 * (level(z, 0) * here - ahead)
        fields[z, 0] = v1[z]
        fields[z, 1] = here
        for i, block in enumerate((inside[z, 0], v1[z], here, half)):
            stack[pl.ds(i * ROWS, ROWS), pl.ds(z * 128, 128)] = block
    pairs = [(add[2, 0], beside[4]), (add[3, 0], beside[5]), (given[0], given[1])]
    pairs.append((beside[2], beside[3]))
    for i, (one, other) in enumerate(pairs):
        seams[pl.ds(0, ROWS), pl.ds(i * 128, 128)] = one
        seams[pl.ds(ROWS, ROWS), pl.ds(i * 128, 128)] = -0.5 * other

    def outer(a, b):
        return lax.dot_general(
            a,
            b,
            (((1,), (1,)), ((), ())),
            precision=lax.Precision.HIGHEST,
            preferred_element_type=jnp.float32,
        )

    gram = outer(stack[...], stack[...])
    seam = outer(seams[...], seams[...])
    seam = jnp.concatenate([jnp.zeros((2 * ROWS, 2 * ROWS), jnp.float32), seam], axis=1)
    lane = lax.broadcasted_iota(jnp.int32, (NB, 128), 1)
    sub = lax.broadcasted_iota(jnp.int32, (NB, 128), 0)
    result = jnp.zeros((NB, 128), jnp.float32)
    blocks = [[(0, 0)], [(0, 1)], [(1, 1)], [(1, 2)], [(2, 2)], [(2, 3), (3, 2)]]
    for n, parts in enumerate(blocks):
        rr = ri = ir = ii = 0.0
        for i, j in parts:
            top = gram[ROWS * i : ROWS * i + NB, :]
            low = gram[ROWS * i + NB : ROWS * i + ROWS, :]
            if n == 5:
                top = top + seam[ROWS * (i - 2) : ROWS * (i - 2) + NB, :]
                low = low + seam[ROWS * (i - 2) + NB : ROWS * (i - 2) + ROWS, :]
            first = (NB * n - ROWS * j) % 128
            second = (NB * n - ROWS * j - NB) % 128
            rr = rr + (pltpu.roll(top, first, 1) if first else top)
            ri = ri + (pltpu.roll(top, second, 1) if second else top)
            ir = ir + (pltpu.roll(low, first, 1) if first else low)
            ii = ii + (pltpu.roll(low, second, 1) if second else low)
        col = lane - NB * n
        inside = (col >= 0) & (col < NB)
        result = jnp.where(inside, jnp.where(col >= sub, rr + ii, ri - ir), result)
        on = col == sub
        m_re = jnp.sum(jnp.where(on, rr - ii, 0.0), axis=1, keepdims=True)
        m_im = jnp.sum(jnp.where(on, ri + ir, 0.0), axis=1, keepdims=True)
        result = jnp.where(lane == 6 * NB + 2 * n, m_re, result)
        result = jnp.where(lane == 6 * NB + 2 * n + 1, m_im, result)
    packed[...] = result


def cmul(a, b):
    return (a[0] * b[0] - a[1] * b[1], a[0] * b[1] + a[1] * b[0])


def cadd(a, b):
    return (a[0] + b[0], a[1] + b[1])


def csub(a, b):
    return (a[0] - b[0], a[1] - b[1])


def cdiv(a, b):
    size = b[0] * b[0] + b[1] * b[1]
    return ((a[0] * b[0] + a[1] * b[1]) / size, (a[1] * b[0] - a[0] * b[1]) / size)


def combine(poles, cells, total, inside, fields, filtered, correlation, energy):
    moments = jnp.sum(total[...], axis=0)
    lane = lax.broadcasted_iota(jnp.int32, (NB, 128), 1)
    m = [
        tuple(
            jnp.broadcast_to(moments[:, 6 * NB + 2 * n + c : 6 * NB + 2 * n + c + 1], (NB, 128))
            for c in (0, 1)
        )
        for n in range(6)
    ]
    cosine = jnp.zeros((NB, 128), jnp.float32)
    sine = jnp.zeros((NB, 128), jnp.float32)
    for j in range(poles):
        angle = 2.0 * math.pi / poles * (j + 0.5)
        cosine = jnp.where(lane == j, math.cos(angle), cosine)
        sine = jnp.where(lane == j, math.sin(angle), sine)
    shift = (contour_center + contour_radius * cosine, contour_radius * sine)
    weight = (contour_radius * cosine / poles, contour_radius * sine / poles)
    zeta = (shift[0] - BASE, shift[1])

    def form(p, q):
        sums = {}
        for i, a in enumerate(p):
            for j, b in enumerate(q):
                ab = cmul(a, b)
                sums[i + j] = cadd(sums[i + j], ab) if i + j in sums else ab
        out = None
        for n, s in sums.items():
            term = cmul(s, m[n])
            out = term if out is None else cadd(out, term)
        return out

    def applied(p):
        q = [cmul(zeta, a) for a in p]
        q = [q[0]] + [csub(q[i], p[i - 1]) for i in range(1, len(p))]
        return q + [(-p[-1][0], -p[-1][1])]

    one = (jnp.ones((NB, 128), jnp.float32), jnp.zeros((NB, 128), jnp.float32))
    residual, direction, solution_ = [one], [one], []
    rho = m[0]
    for iteration in range(3):
        q = applied(direction)
        alpha = cdiv(rho, form(direction, q))
        step = [cmul(alpha, d) for d in direction]
        solution_ = [cadd(s, t) for s, t in zip(solution_, step)] + step[len(solution_) :]
        step = [cmul(alpha, d) for d in q]
        residual = [csub(r, t) for r, t in zip(residual, step)] + [
            (-t[0], -t[1]) for t in step[len(residual) :]
        ]
        if iteration < 2:
            rho_new = form(residual, residual)
            beta = cdiv(rho_new, rho)
            step = [cmul(beta, d) for d in direction]
            direction = [cadd(r, t) for r, t in zip(residual, step)] + residual[len(step) :]
            rho = rho_new
    image = []
    for k in range(4):
        term = residual[k]
        if k < 3:
            term = cadd(term, cmul(shift, solution_[k]))
        if k == 0:
            term = (term[0] - 1.0, term[1])
        image.append(term)

    def over_poles(term):
        term = cmul(weight, term)
        return tuple(
            jnp.sum(jnp.where(lane < poles, t, 0.0), axis=1, keepdims=True) for t in term
        )

    coef = [over_poles(s) for s in solution_]
    coef_image = [over_poles(s) for s in image]
    for z in range(NZ):
        re = im = 0.0
        for k in range(3):
            v = inside[z, 0] if k == 0 else fields[z, k - 1]
            v_re, v_im = v[:NB], v[NB:]
            re = re + (coef[k][0] * v_re - coef[k][1] * v_im)
            im = im + (coef[k][0] * v_im + coef[k][1] * v_re)
        filtered[0, :, z, :] = re
        filtered[1, :, z, :] = im

    a = lax.broadcasted_iota(jnp.int32, (NB, NB), 0)
    b = lax.broadcasted_iota(jnp.int32, (NB, NB), 1)
    flipped = lax.dot_general(
        moments,
        jnp.where(a == b, 1.0, 0.0),
        (((0,), (0,)), ((), ())),
        precision=lax.Precision.HIGHEST,
        preferred_element_type=jnp.float32,
    )
    inner = []
    for n in range(6):
        here = moments[:, NB * n : NB * n + NB]
        there = flipped[NB * n : NB * n + NB, :]
        inner.append(
            (
                jnp.where(b >= a, here, there),
                jnp.where(b < a, here, jnp.where(b > a, -there, 0.0)),
            )
        )

    def as_row(c):
        return tuple(
            jnp.sum(jnp.where(a == b, jnp.broadcast_to(t, (NB, NB)), 0.0), axis=0, keepdims=True)
            for t in c
        )

    def product(right, out):
        rows = [as_row(c) for c in right]
        result = None
        for k in range(3):
            part = None
            for l, r in enumerate(rows):
                term = cmul(r, inner[k + l])
                part = term if part is None else cadd(part, term)
            term = cmul((coef[k][0], -coef[k][1]), part)
            result = term if result is None else cadd(result, term)
        out[0] = result[0] * (1.0 / cells)
        out[1] = result[1] * (1.0 / cells)

    product(coef, correlation)
    product(coef_image, energy)


def call(kernel, out, scratch, *operands, flops=1 << 20):
    space = {"s": pltpu.SMEM, "h": pltpu.HBM, "v": pltpu.VMEM}
    return pl.pallas_call(
        kernel,
        in_specs=[pl.BlockSpec(memory_space=space[kind]) for kind, _ in operands],
        out_specs=[pl.BlockSpec(memory_space=pltpu.VMEM)] * len(out),
        out_shape=[jax.ShapeDtypeStruct(shape, jnp.float32) for shape in out],
        scratch_shapes=scratch,
        compiler_params=pltpu.CompilerParams(vmem_limit_bytes=8 << 20),
        cost_estimate=pl.CostEstimate(flops=flops, bytes_accessed=1 << 19, transcendentals=0),
        name=getattr(kernel, "__name__", "combine"),
    )(*[operand for _, operand in operands])


def on_device(vectors, potential):
    vectors = pltpu.with_memory_space_constraint(vectors, pltpu.HBM)
    potential = pltpu.with_memory_space_constraint(potential, pltpu.HBM)
    row = own_row().reshape(1).astype(jnp.int32)

    def scratch(rows):
        slots = sum(map(len, rows.values()))
        return [
            pltpu.VMEM((slots, 2, NB, 128), jnp.float32),
            pltpu.VMEM(potential.shape, jnp.float32),
            pltpu.SemaphoreType.DMA((slots + 1,)),
        ]

    source = (("s", row), ("h", vectors), ("h", potential))
    up, down = call(
        slab_edges, [(5 * ROWS + 16, 128), (2 * ROWS, 128)], scratch(EDGE), *source
    )
    slabs = lax.axis_size(SLAB)
    below = lax.ppermute(up, SLAB, [(i, (i + 1) % slabs) for i in range(slabs)])
    above = lax.ppermute(down, SLAB, [(i, (i - 1) % slabs) for i in range(slabs)])
    inside, beside, diagonals = call(
        slab_fields,
        [(NZ, 4, ROWS, 128), (6, ROWS, 128), (2 * NZ, 128)],
        scratch(WIDE),
        *source,
    )
    packed, fields = call(
        krylov_gram,
        [(NB, 128), (NZ, 2, ROWS, 128)],
        [pltpu.VMEM((rows * ROWS, NZ * 128), jnp.float32) for rows in (4, 2)],
        *(("v", a) for a in (inside, beside, diagonals, below, above)),
    )
    for axes in PHASES:
        count = lax.axis_size(axes)
        shared = jnp.broadcast_to(packed[None], (count, NB, 128))
        received = lax.all_to_all(shared, axes, 0, 0)
        packed = received if axes == PHASES[-1] else jnp.sum(received, axis=0)
    cells = NZ * slabs * NX * 128
    filtered, correlation, energy = call(
        functools.partial(combine, lax.axis_size(POLE), cells),
        [(2, NB, NZ, 128), (2, NB, NB), (2, NB, NB)],
        [],
        *(("v", a) for a in (packed, inside, fields)),
    )
    return filtered[:, :, :, None, :], correlation, energy


def solution(mesh):
    fine = Mesh(mesh.devices.reshape(4, 2, 2, 8, 4), POLE + SLAB)
    in_specs = (P(None, None, SLAB, None, None), P(SLAB, None, None))
    out_specs = (P(None, None, SLAB, POLE, None), P(), P())
    return jax.shard_map(
        on_device, mesh=fine, in_specs=in_specs, out_specs=out_specs, check_vma=False
    )
```
